1024 devices in a mesh: dp: 8 (over y), ctx: 32 (over z, core), tensor: 4 (over x).
Axes of the slice: x: 4, y: 8, z: 16, core: 2. Of those that a mesh axis runs over, the one named last changes fastest.
Arguments:
- mamba_input: bfloat16 [32768, 4096], P(('dp', 'ctx'), 'tensor'), parts along dimension 0, may hold values from -140 to 140
- mamba_gate: bfloat16 [32768, 4096], P(('dp', 'ctx'), 'tensor'), parts along dimension 0, may hold values from -6 to 6
- state_write: bfloat16 [32768, 512], P(('dp', 'ctx'), 'tensor'), parts along dimension 0, may hold values from -1.796875 to 1.796875
- state_read: bfloat16 [32768, 512], P(('dp', 'ctx'), 'tensor'), parts along dimension 0, may hold values from -1.796875 to 1.796875
- step_size: float32 [32768, 64], P(('dp', 'ctx'), 'tensor'), parts along dimension 0, may hold values from 0.25 to 4
- decay_rate: float32 [64], P('tensor'), may hold values from 4.8828125e-05 to 0.034
- skip_scale: float32 [64], P('tensor'), may hold values from 1 to 8
- norm_gain: float32 [4096], P('tensor'), may hold values from 0.5 to 1.5
- query_rows: bfloat16 [32768, 2048], P(('dp', 'ctx'), 'tensor'), parts along dimension 0, may hold values from -10 to 10
- key_rows: bfloat16 [32768, 512], P(('dp', 'ctx'), 'tensor'), parts along dimension 0, may hold values from -10 to 10
- value_rows: bfloat16 [32768, 512], P(('dp', 'ctx'), 'tensor'), parts along dimension 0, may hold values from -6 to 6
- doc_offsets: int32 [264], P('dp'), parts along dimension 0, may hold values from 0 to 4096, as said below
Outputs:
- mamba_out: bfloat16 [32768, 4096], P(('dp', 'ctx'), 'tensor'), parts along dimension 0
- attn_out: bfloat16 [32768, 2048], P(('dp', 'ctx'), 'tensor'), parts along dimension 0
The draws below stay inside these ranges and needn't reach their ends.
There are 8 independent parts, one for each index of `dp`. The reference program is written for one: setup_inputs(seed, part) draws one part's arguments, and reference() takes and returns one part's arrays. A program takes and returns all parts, laid end to end along the dimension named above; an argument that names none is the same for every part. Nothing has to cross between parts.
Inputs may be any that keep to these rules, and one draw needn't show every extreme that they name: doc_offsets[0] is 0 and doc_offsets[32] is 4096; the offsets rise strictly; every document holds 1 to 3072 tokens and one holds exactly 3072.
All inputs are finite; a program needn't handle non-finite values.
Results may differ from the reference program's by a relative error of at most 0.0085.
Values may be sent and summed in bfloat16 or wider, within the bound.
A program may use at most 64 MiB of HBM per device.

```python
import math
import jax
import jax.numpy as jnp
from jax import lax

MH = 64
MP = 64
MN = 128
MG = 4
QH = 16
KVH = 4
HD = 128
TOK_DEV = 128
TOKENS = 4096
DOCS = 32
MOST = 3072


def document_offsets(key):
    first_key, second_key = jax.random.split(jax.random.fold_in(key, 7001))
    remain = TOKENS - MOST
    shuffled = jax.random.permutation(first_key, remain - 1) + 1
    cuts = jnp.sort(shuffled[:DOCS - 2]).astype(jnp.int32)
    edges = jnp.concatenate([jnp.zeros((1,), jnp.int32), cuts, jnp.full((1,), remain, jnp.int32)])
    pieces = edges[1:] - edges[:-1]
    chosen = jax.random.randint(second_key, (), 0, DOCS)
    slots = jnp.arange(DOCS, dtype=jnp.int32)
    source = jnp.clip(slots - (slots > chosen).astype(jnp.int32), 0, DOCS - 2)
    lengths = jnp.where(slots == chosen, MOST, pieces[source]).astype(jnp.int32)
    offsets = jnp.concatenate([jnp.zeros((1,), jnp.int32), jnp.cumsum(lengths).astype(jnp.int32)])
    return offsets


def draw_doc_offsets(key, part):
    return document_offsets(key)


def draw_query_rows(key, part):
    base = jax.random.truncated_normal(jax.random.fold_in(key, 7003), -6.0, 6.0, (TOKENS, QH * HD), jnp.float32)
    return base.astype(jnp.bfloat16)


def draw_key_rows(key, part):
    base = jax.random.truncated_normal(jax.random.fold_in(key, 7004), -6.0, 6.0, (TOKENS, KVH * HD), jnp.float32)
    return base.astype(jnp.bfloat16)


def draw_mamba_input(key, part):
    row_key, col_key, base_key = jax.random.split(jax.random.fold_in(key, 7005), 3)
    row_scale = jnp.exp(jax.random.uniform(row_key, (TOKENS, 1), jnp.float32, 0.0, math.log(10.0)))
    col_scale = jnp.exp(jax.random.uniform(col_key, (1, MH * MP), jnp.float32, 0.0, math.log(10.0)))
    base = jax.random.truncated_normal(base_key, -4.0, 4.0, (TOKENS, MH * MP), jnp.float32)
    return (base * row_scale * col_scale / 3.0).astype(jnp.bfloat16)


def draw_decay_rate(key, part):
    fast_key, slow_key, quick_key = jax.random.split(jax.random.fold_in(key, 7006), 3)
    share = 0.5
    fast = jax.random.bernoulli(fast_key, share, (MH,))
    slow_rate = jnp.exp(jax.random.uniform(slow_key, (MH,), jnp.float32, math.log(0.2 / TOKENS), math.log(0.5 / TOKENS)))
    quick_rate = jnp.exp(jax.random.uniform(quick_key, (MH,), jnp.float32, math.log(1.0 / 50.0), math.log(1.0 / 30.0)))
    return jnp.where(fast, quick_rate, slow_rate).astype(jnp.float32)


def draw_step_size(key, part):
    local_key, block_key = jax.random.split(jax.random.fold_in(key, 7007))
    local = jnp.exp(jax.random.uniform(local_key, (TOKENS, MH), jnp.float32, math.log(0.5), math.log(2.0)))
    blocks = jnp.exp(jax.random.uniform(block_key, (TOKENS // TOK_DEV, 1), jnp.float32, math.log(0.5), math.log(2.0)))
    return (local * jnp.repeat(blocks, TOK_DEV, axis=0)).astype(jnp.float32)


def steps_of(rng, dims, shards, least, largest):
    loudness, own = 1.0, jax.random.fold_in(rng, 6)
    for position, shards_of in shards:
        heights = jnp.exp(jax.random.uniform(jax.random.fold_in(own, position), (shards_of,), jnp.float32, least / len(shards), largest / len(shards)))
        loudness = loudness * jnp.repeat(heights, dims[position] // shards_of).reshape([-1 if axis == position else 1 for axis in range(len(dims))])
    return loudness


def centred(key, extent, width, bound, shards=(), kind=jnp.bfloat16):
    drawn = jax.random.normal(key, extent, jnp.float32) * width
    if len(shards) > 0:
        drawn = steps_of(key, extent, shards, -0.22, 0.18) * drawn
    return jnp.clip(drawn, min=-bound, max=bound).astype(kind)


def setup_inputs(seed: int = 0, part: int = 0) -> dict:
    keys = jax.random.split(jax.random.key(seed), 13)
    own_keys = jax.random.split(jax.random.fold_in(keys[12], part), 13)
    return {
        "mamba_input": draw_mamba_input(jax.random.fold_in(jax.random.fold_in(keys[12], part), 71), part),
        "mamba_gate": centred(own_keys[1], (TOKENS, MH * MP), 1.0, 6.0, ((0, 32), (1, 4))),
        "state_write": centred(own_keys[2], (TOKENS, MG * MN), 0.3, 1.796875, ((0, 32), (1, 4))),
        "state_read": centred(own_keys[3], (TOKENS, MG * MN), 0.3, 1.796875, ((0, 32), (1, 4))),
        "step_size": draw_step_size(jax.random.fold_in(jax.random.fold_in(keys[12], part), 71), part),
        "decay_rate": draw_decay_rate(jax.random.fold_in(keys[12], 71), part),
        "skip_scale": jnp.clip(jnp.exp(math.log(8.0) - 2.0794415 * jax.random.uniform(keys[6], (MH,), jnp.float32) ** steps_of(keys[6], (MH,), ((0, 4),), -0.2, 0.2)), 1.0, 8.0),
        "norm_gain": jnp.clip(1.0 + 0.1 * jax.random.normal(keys[7], (MH * MP,), jnp.float32), 0.5, 1.5),
        "query_rows": draw_query_rows(jax.random.fold_in(jax.random.fold_in(keys[12], part), 71), part),
        "key_rows": draw_key_rows(jax.random.fold_in(jax.random.fold_in(keys[12], part), 71), part),
        "value_rows": centred(own_keys[10], (TOKENS, KVH * HD), 1.0, 6.0, ((0, 32), (1, 4))),
        "doc_offsets": draw_doc_offsets(jax.random.fold_in(jax.random.fold_in(keys[12], part), 71), part),
    }


def doc_index(positions, doc_offsets):
    interior = doc_offsets[1:-1]
    return lax.optimization_barrier(jnp.sum((positions[:, None] >= interior[None, :]).astype(jnp.int32), axis=1))

def doc_first(positions, doc_offsets):
    return jnp.any(positions[:, None] == doc_offsets[None, :-1], axis=1)

def reference(mamba_input, mamba_gate, state_write, state_read, step_size, decay_rate, skip_scale, norm_gain, query_rows, key_rows, value_rows, doc_offsets):
    positions = jnp.arange(TOKENS, dtype=jnp.int32)
    first = doc_first(positions, doc_offsets)
    per_group = MH // MG
    group_of = jnp.arange(MH, dtype=jnp.int32) // per_group
    inputs = mamba_input.astype(jnp.float32).reshape(TOKENS, MH, MP)
    writes = state_write.astype(jnp.float32)
    reads = state_read.astype(jnp.float32)
    decay = jnp.where(first[:, None], jnp.float32(0.0), jnp.exp(-decay_rate[None, :] * step_size))

    def advance(state, packed):
        x_row, write_row, read_row, step_row, decay_row = packed
        write_head = write_row.reshape(MG, MN)[group_of]
        read_head = read_row.reshape(MG, MN)[group_of]
        state = decay_row[:, None, None] * state + (step_row[:, None] * write_head)[:, :, None] * x_row[:, None, :]
        output = jnp.einsum('hn,hnp->hp', read_head, state, precision=lax.Precision.HIGHEST)
        return (state, output)
    start_state = jnp.zeros((MH, MN, MP), jnp.float32)
    _, mixed = lax.scan(advance, start_state, (inputs, writes, reads, step_size, decay))
    mixed = mixed + skip_scale[None, :, None] * inputs
    gated = mixed * jax.nn.silu(mamba_gate.astype(jnp.float32).reshape(TOKENS, MH, MP))
    grouped = gated.reshape(TOKENS, MG, per_group * MP)
    normed = grouped * lax.rsqrt(lax.optimization_barrier(jnp.mean(grouped * grouped, axis=-1, keepdims=True)) + 1e-05)
    mamba_out = (normed.reshape(TOKENS, MH * MP) * norm_gain[None, :]).astype(jnp.bfloat16)
    doc_ids = doc_index(positions, doc_offsets)
    per_kv = QH // KVH
    block = math.gcd(TOKENS, 256)
    keys_full = key_rows.astype(jnp.float32).reshape(TOKENS, KVH, HD)
    values_full = value_rows.astype(jnp.float32).reshape(TOKENS, KVH, HD)

    def one_block(index):
        begin = (index * block).astype(jnp.int32)
        queries = lax.dynamic_slice_in_dim(query_rows, begin, block, 0).astype(jnp.float32).reshape(block, KVH, per_kv, HD)
        query_pos = begin + jnp.arange(block, dtype=jnp.int32)
        query_doc = lax.dynamic_slice_in_dim(doc_ids, begin, block, 0)
        scores = jnp.einsum('tgqd,sgd->gqts', queries, keys_full, precision=lax.Precision.HIGHEST) / math.sqrt(HD)
        visible = (doc_ids[None, :] == query_doc[:, None]) & (positions[None, :] <= query_pos[:, None])
        scores = jnp.where(visible[None, None], scores, jnp.float32(-1e+30))
        top = lax.optimization_barrier(jnp.max(scores, axis=-1, keepdims=True))
        expo = jnp.where(visible[None, None], jnp.exp(scores - top), jnp.float32(0.0))
        weights = lax.optimization_barrier(expo.astype(jnp.bfloat16)).astype(jnp.float32)
        numer = jnp.einsum('gqts,sgd->tgqd', weights, values_full, precision=lax.Precision.HIGHEST)
        denom = lax.optimization_barrier(jnp.sum(expo, axis=-1)).transpose(2, 0, 1)
        result = numer / denom[:, :, :, None]
        return result.reshape(block, QH * HD).astype(jnp.bfloat16)
    attn_out = lax.map(one_block, jnp.arange(TOKENS // block, dtype=jnp.int32)).reshape(TOKENS, QH * HD)
    return (mamba_out, attn_out)
```

```python
import functools
import math

import jax
import jax.numpy as jnp
from jax import lax
from jax.experimental import pallas as pl
from jax.experimental.pallas import tpu as pltpu
from jax.sharding import PartitionSpec as P

MESH = pl.DeviceIdType.MESH
HIGHEST = lax.Precision.HIGHEST
F32, BF16 = jnp.float32, jnp.bfloat16

MP = 64
HD = 128
TOK = 128
CHIPS = 16
HEADS = 16
COLS = HEADS * MP
TILES = COLS // 128
NEAR = 7
FAR = 12
NEG = -1e30
SCALE = math.log2(math.e) / math.sqrt(HD)


def nt_dot(a, b):
    return lax.dot_general(a, b, (((1,), (1,)), ((), ())), preferred_element_type=F32)


def tn_dot(a, b):
    return lax.dot_general(a, b, (((0,), (0,)), ((), ())), preferred_element_type=F32)


def spread(table, tile):
    rows = table.shape[0]
    lane = lax.broadcasted_iota(jnp.int32, (rows, 128), 1)
    return jnp.where(lane < MP, table[:, 2 * tile : 2 * tile + 1], table[:, 2 * tile + 1 : 2 * tile + 2])


def kernel(
    offs_ref,
    step_ref,
    rate_ref,
    skip_ref,
    gain_ref,
    x_hbm,
    gate_hbm,
    write_hbm,
    read_hbm,
    q_hbm,
    k_hbm,
    v_hbm,
    mamba_ref,
    attn_ref,
    x_ref,
    gate_ref,
    b_ref,
    c_ref,
    q_ref,
    kv_ref,
    u_ref,
    lhs_ref,
    er_ref,
    own_ref,
    own_send,
    part_ref,
    thr_own,
    thr_part,
    comb_ref,
    comb_thr,
    in1_ref,
    thr1_ref,
    pre_ref,
    in2_ref,
    state_ref,
    other_ref,
    start_ref,
    qpos_ref,
    top_ref,
    acc_ref,
    gated_ref,
    load_sem,
    near_recv,
    pair_recv,
    near_send,
    pair_send,
    ex_send,
    ex_recv,
    s1_send,
    s1_recv,
    t1_send,
    t1_recv,
    s2_send,
    s2_recv,
):
    me = lax.axis_index("ctx")
    z, core = lax.div(me, 2), lax.rem(me, 2)
    partner = me + 1 - 2 * core
    anchor = me * TOK

    def chip(index):
        return {"ctx": 2 * index + core}

    def remote(src, dst, send, recv, device):
        return pltpu.make_async_remote_copy(
            src_ref=src, dst_ref=dst, send_sem=send, recv_sem=recv, device_id=device, device_id_type=MESH
        )

    def peer(k):
        turn = lax.div(k + 1, 2)
        away = CHIPS // 2 + jnp.where(lax.rem(k, 2) == 1, turn, -turn)
        return lax.rem(z + away, CHIPS)

    barrier = pltpu.get_barrier_semaphore()

    def greet(k, _):
        pl.semaphore_signal(barrier, inc=1, device_id=chip(peer(k)), device_id_type=MESH)
        return 0

    lax.fori_loop(0, CHIPS - 1, greet, 0)
    pl.semaphore_signal(barrier, inc=1, device_id={"ctx": partner}, device_id_type=MESH)

    loads = [
        pltpu.make_async_copy(src, dst, load_sem.at[n])
        for n, (src, dst) in enumerate(
            (
                (k_hbm, kv_ref.at[0, core, 0]),
                (v_hbm, kv_ref.at[0, core, 1]),
                (write_hbm, b_ref),
                (read_hbm, c_ref),
                (x_hbm, x_ref),
                (q_hbm, q_ref),
                (gate_hbm, gate_ref),
            )
        )
    ]
    for load in loads:
        load.start()

    row = lax.broadcasted_iota(jnp.int32, (TOK, 128), 0)
    col = lax.broadcasted_iota(jnp.int32, (TOK, 128), 1)
    pos = anchor + row
    start = jnp.zeros((TOK, 128), jnp.int32)
    final = jnp.zeros((8, 128), jnp.int32)
    for d in range(1, 32):
        off = offs_ref[d]
        start = jnp.where(pos >= off, off, start)
        final = jnp.where(anchor + TOK - 1 + jnp.zeros((8, 128), jnp.int32) >= off, off, final)
    final = final[0:1]
    start_ref[...] = start
    qpos_ref[...] = pos

    lower = (col <= row).astype(F32)
    running = jnp.dot(lower, -rate_ref[...] * step_ref[...], precision=HIGHEST, preferred_element_type=F32)
    grow = jnp.exp(-running) * step_ref[...]
    er_ref[...] = jnp.exp(running)
    last = jnp.exp(running[TOK - 1 : TOK])

    for load in loads[:5]:
        load.wait()
    held = jnp.where(pos >= final, b_ref[...].astype(F32), 0.0)
    held_t = held.T.astype(BF16)
    inner = jnp.where((col <= row) & (anchor + col >= start), nt_dot(c_ref[...], b_ref[...]), 0.0)
    entering = jnp.where(start < anchor, c_ref[...].astype(F32), 0.0)
    lhs_ref[:, 0:128] = inner.astype(BF16)
    lhs_ref[:, 128:256] = entering.astype(BF16)
    for t in range(TILES):
        sl = slice(128 * t, 128 * t + 128)
        u = (x_ref[:, sl].astype(F32) * spread(grow, t)).astype(BF16)
        u_ref[:, sl] = u
        decay = spread(last, t)
        tile = jnp.dot(held_t, u, preferred_element_type=F32) * decay
        own_ref[4 * t : 4 * t + 4] = tile.reshape(4, 32, 128)
        own_send[4 * t : 4 * t + 4] = tile.astype(BF16).reshape(4, 32, 128)
        thr_own[t] = jnp.where(final < anchor, decay, 0.0)

    pl.semaphore_wait(barrier, CHIPS)

    def forward(d):
        return remote(kv_ref.at[d, core], kv_ref.at[d + 1, core], near_send.at[d], near_recv.at[d + 1], chip(z + 1))

    def backward(d):
        return remote(kv_ref.at[d, core], kv_ref.at[d - 1, core], near_send.at[d], near_recv.at[d - 1], chip(z - 1))

    def direct():
        target = jnp.minimum(z + FAR, CHIPS - 1)
        return remote(
            kv_ref.at[0, core], kv_ref.at[target - z, core], near_send.at[NEAR], near_recv.at[target - z], chip(target)
        )

    def pair(d):
        return remote(kv_ref.at[d, core], kv_ref.at[d, core], pair_send.at[d], pair_recv.at[d], {"ctx": partner})

    @pl.when(z < CHIPS - 1)
    def _():
        forward(0).start()

    @pl.when(z + NEAR < CHIPS - 1)
    def _():
        direct().start()

    pair(0).start()

    ex_state = remote(
        own_send.at[pl.ds(16 * (1 - core), 16)], part_ref, ex_send.at[0], ex_recv.at[0], {"ctx": partner}
    )
    ex_thr = remote(thr_own, thr_part, ex_send.at[1], ex_recv.at[1], {"ctx": partner})
    ex_state.start()
    ex_thr.start()
    ex_thr.wait_recv()
    ex_state.wait_recv()
    is_first = core == 0
    for t in range(4):
        own = own_ref[pl.ds(16 * core + 4 * t, 4)]
        part = part_ref[4 * t : 4 * t + 4].astype(F32)
        mine, theirs = thr_own[4 * core + t], thr_part[4 * core + t]
        early, late = jnp.where(is_first, own, part), jnp.where(is_first, part, own)
        comb = jnp.where(is_first, theirs, mine)[None] * early + late
        comb_ref[4 * t : 4 * t + 4] = comb.astype(BF16)
        comb_thr[4 * t : 4 * t + 4] = jnp.broadcast_to((mine * theirs)[None], (4, 1, 128))

    def s1(target, source):
        return remote(comb_ref.at[target], in1_ref.at[source], s1_send.at[target], s1_recv.at[source], chip(target))

    def t1(target, source):
        return remote(comb_thr.at[target], thr1_ref.at[source], t1_send.at[target], t1_recv.at[source], chip(target))

    def s2(target, source):
        return remote(pre_ref.at[target], in2_ref.at[source], s2_send.at[target], s2_recv.at[source], chip(target))

    def send1(k, _):
        s1(peer(k), z).start()
        t1(peer(k), z).start()
        return 0

    lax.fori_loop(0, CHIPS - 1, send1, 0)
    in1_ref[z] = comb_ref[z]
    thr1_ref[z] = comb_thr[z]

    for load in loads[5:]:
        load.wait()
    top_ref[...] = jnp.full(top_ref.shape, NEG, F32)
    acc_ref[...] = jnp.zeros(acc_ref.shape, F32)
    heads = q_ref.shape[1] // HD

    def attend(d, causal):
        keys = jnp.concatenate([kv_ref[d, 0, 0], kv_ref[d, 1, 0]], axis=0)
        values = jnp.concatenate([kv_ref[d, 0, 1], kv_ref[d, 1, 1]], axis=0)
        values = jnp.concatenate([values, jnp.ones((2 * TOK, 128), BF16)], axis=1)
        lane = (z - d) * (2 * TOK) + lax.broadcasted_iota(jnp.int32, (TOK, 2 * TOK), 1)
        begin = start_ref[...]
        seen = lane >= jnp.concatenate([begin, begin], axis=1)
        if causal:
            here = qpos_ref[...]
            seen = seen & (lane <= jnp.concatenate([here, here], axis=1))
        for h in range(heads):
            scores = nt_dot(q_ref[:, h * HD : (h + 1) * HD], keys) * SCALE
            scores = jnp.where(seen, scores, NEG)
            before = top_ref[h]
            top = jnp.maximum(before, jnp.max(scores, axis=1, keepdims=True))
            top_ref[h] = top
            fade = jnp.exp2(before - top)
            weights = jnp.exp2(scores - jnp.concatenate([top, top], axis=1)).astype(BF16)
            update = jnp.dot(weights, values, preferred_element_type=F32)
            acc_ref[h] = acc_ref[h] * jnp.concatenate([fade, fade], axis=1) + update

    pair(0).wait_recv()
    attend(0, True)

    def scan():
        def arrive(k, _):
            s1(z, peer(k)).wait_recv()
            t1(z, peer(k)).wait_recv()
            return 0

        lax.fori_loop(0, CHIPS - 1, arrive, 0)
        prefix = jnp.zeros((32, 128), F32)
        for j in range(CHIPS):
            pre_ref[j] = prefix.astype(BF16)
            prefix = thr1_ref[j] * prefix + in1_ref[j].astype(F32)

        def send2(k, _):
            s2(peer(k), z).start()
            return 0

        lax.fori_loop(0, CHIPS - 1, send2, 0)
        in2_ref[z] = pre_ref[z]

    def block(d):
        pair(d).wait_recv()
        attend(d, False)

    def near_arrive(d):
        @pl.when(z >= d)
        def _():
            remote(kv_ref.at[d, core], kv_ref.at[d, core], near_send.at[d], near_recv.at[d], chip(z - d)).wait_recv()

            @pl.when((d < NEAR) & (z < CHIPS - 1))
            def _():
                forward(d).start()

            @pl.when(d > NEAR + 1)
            def _():
                backward(d).start()

            pair(d).start()

    def step(d, _):
        far = FAR + 2 - d

        @pl.when(d <= NEAR)
        def _():
            near_arrive(d)

        @pl.when((far > NEAR) & (far <= FAR))
        def _():
            near_arrive(far)

        @pl.when(d == 4)
        def _():
            scan()

        def late(n, _):
            e = jnp.where(n == 0, d - 1, far + 1)

            @pl.when((e >= 1) & (e <= FAR) & (z >= e) & ((n == 0) | (e > NEAR)))
            def _():
                block(e)

            return 0

        lax.fori_loop(0, 2, late, 0)
        return 0

    lax.fori_loop(1, NEAR + 2, step, 0)

    def arrive2(k, _):
        s2(z, peer(k)).wait_recv()
        return 0

    lax.fori_loop(0, CHIPS - 1, arrive2, 0)
    for t in range(4):
        own = own_ref[pl.ds(16 * core + 4 * t, 4)]
        part = part_ref[4 * t : 4 * t + 4].astype(F32)
        mine, theirs = thr_own[4 * core + t], thr_part[4 * core + t]
        chip_in = in2_ref[4 * t : 4 * t + 4].astype(F32)
        second = jnp.where(is_first, mine, theirs)[None] * chip_in + jnp.where(is_first, own, part)
        state_ref[pl.ds(16 * core + 4 * t, 4)] = jnp.where(is_first, chip_in, second).astype(BF16)
        other_ref[4 * t : 4 * t + 4] = jnp.where(is_first, second, chip_in).astype(BF16)
    half = pl.ds(16 * core, 16)
    theirs_half = pl.ds(16 * (1 - core), 16)
    ex_back = remote(other_ref, state_ref.at[half], ex_send.at[2], ex_recv.at[2], {"ctx": partner})
    ex_back.start()
    for h in range(heads):
        attn_ref[:, h * HD : (h + 1) * HD] = (acc_ref[h, :, 0:HD] / acc_ref[h, :, HD : 2 * HD]).astype(BF16)
    remote(other_ref, state_ref.at[theirs_half], ex_send.at[2], ex_recv.at[2], {"ctx": partner}).wait_recv()

    square = jnp.zeros((TOK, 128), F32)
    er = er_ref[...]
    skip = skip_ref[...]
    for t in range(TILES):
        sl = slice(128 * t, 128 * t + 128)
        rhs = jnp.concatenate([u_ref[:, sl], state_ref[4 * t : 4 * t + 4].reshape(128, 128)], axis=0)
        mixed = jnp.dot(lhs_ref[...], rhs, preferred_element_type=F32) * spread(er, t)
        mixed = mixed + spread(skip, t) * x_ref[:, sl].astype(F32)
        gate = gate_ref[:, sl].astype(F32)
        gated = mixed * (gate / (1.0 + jnp.exp(-gate)))
        gated_ref[:, sl] = gated
        square = square + gated * gated
    norm = lax.rsqrt(jnp.sum(square, axis=1, keepdims=True) * (1.0 / COLS) + 1e-05)
    for t in range(TILES):
        sl = slice(128 * t, 128 * t + 128)
        mamba_ref[:, sl] = (gated_ref[:, sl] * norm * gain_ref[:, sl]).astype(BF16)

    ex_state.wait_send()
    ex_thr.wait_send()
    ex_back.wait_send()

    def sent(k, _):
        s1(peer(k), z).wait_send()
        t1(peer(k), z).wait_send()
        s2(peer(k), z).wait_send()
        return 0

    lax.fori_loop(0, CHIPS - 1, sent, 0)

    @pl.when(z + NEAR < CHIPS - 1)
    def _():
        direct().wait_send()

    def relayed(d, _):
        @pl.when(z >= d)
        def _():
            @pl.when((d < NEAR) & (z < CHIPS - 1))
            def _():
                forward(d).wait_send()

            @pl.when(d > NEAR + 1)
            def _():
                backward(d).wait_send()

            pair(d).wait_send()

        return 0

    lax.fori_loop(0, FAR + 1, relayed, 0)


def per_device(
    mamba_input,
    mamba_gate,
    state_write,
    state_read,
    step_size,
    decay_rate,
    skip_scale,
    norm_gain,
    query_rows,
    key_rows,
    value_rows,
    doc_offsets,
):
    vmem, hbm = pl.BlockSpec(memory_space=pltpu.VMEM), pl.BlockSpec(memory_space=pl.ANY)
    dma = pltpu.SemaphoreType.DMA
    heads = query_rows.shape[1] // HD
    return pl.pallas_call(
        kernel,
        out_shape=(
            jax.ShapeDtypeStruct(mamba_input.shape, BF16),
            jax.ShapeDtypeStruct(query_rows.shape, BF16),
        ),
        in_specs=[pl.BlockSpec(memory_space=pltpu.SMEM)] + [vmem] * 4 + [hbm] * 7,
        out_specs=(vmem, vmem),
        scratch_shapes=[
            pltpu.VMEM((TOK, COLS), BF16),
            pltpu.VMEM((TOK, COLS), BF16),
            pltpu.VMEM((TOK, 128), BF16),
            pltpu.VMEM((TOK, 128), BF16),
            pltpu.VMEM((TOK, heads * HD), BF16),
            pltpu.VMEM((FAR + 1, 2, 2, TOK, HD), BF16),
            pltpu.VMEM((TOK, COLS), BF16),
            pltpu.VMEM((TOK, 256), BF16),
            pltpu.VMEM((TOK, HEADS), F32),
            pltpu.VMEM((32, 32, 128), F32),
            pltpu.VMEM((32, 32, 128), BF16),
            pltpu.VMEM((16, 32, 128), BF16),
            pltpu.VMEM((TILES, 1, 128), F32),
            pltpu.VMEM((TILES, 1, 128), F32),
            pltpu.VMEM((CHIPS, 32, 128), BF16),
            pltpu.VMEM((CHIPS, 1, 128), F32),
            pltpu.VMEM((CHIPS, 32, 128), BF16),
            pltpu.VMEM((CHIPS, 1, 128), F32),
            pltpu.VMEM((CHIPS, 32, 128), BF16),
            pltpu.VMEM((CHIPS, 32, 128), BF16),
            pltpu.VMEM((32, 32, 128), BF16),
            pltpu.VMEM((16, 32, 128), BF16),
            pltpu.VMEM((TOK, 128), jnp.int32),
            pltpu.VMEM((TOK, 128), jnp.int32),
            pltpu.VMEM((heads, TOK, 128), F32),
            pltpu.VMEM((heads, TOK, 256), F32),
            pltpu.VMEM((TOK, COLS), F32),
            dma((7,)),
            dma((FAR + 1,)),
            dma((FAR + 1,)),
            dma((FAR + 1,)),
            dma((FAR + 1,)),
            dma((3,)),
            dma((3,)),
            dma((CHIPS,)),
            dma((CHIPS,)),
            dma((CHIPS,)),
            dma((CHIPS,)),
            dma((CHIPS,)),
            dma((CHIPS,)),
        ],
        compiler_params=pltpu.CompilerParams(collective_id=0, has_side_effects=True, vmem_limit_bytes=48 << 20),
    )(
        doc_offsets,
        step_size,
        decay_rate.reshape(1, -1),
        skip_scale.reshape(1, -1),
        norm_gain.reshape(1, -1),
        mamba_input,
        mamba_gate,
        state_write,
        state_read,
        query_rows,
        key_rows,
        value_rows,
    )


def solution(mesh):
    rows, cols = P(("dp", "ctx"), "tensor"), P("tensor")
    return jax.shard_map(
        per_device,
        mesh=mesh,
        in_specs=(rows,) * 5 + (cols,) * 3 + (rows,) * 3 + (P("dp"),),
        out_specs=(rows, rows),
        check_vma=False,
    )
```

```python
import functools
import math

import jax
import jax.numpy as jnp
from jax import lax
from jax.experimental import pallas as pl
from jax.experimental.pallas import tpu as pltpu
from jax.sharding import PartitionSpec as P

MESH = pl.DeviceIdType.MESH
HIGHEST = lax.Precision.HIGHEST
F32, BF16 = jnp.float32, jnp.bfloat16

MP = 64
HD = 128
TOK = 128
CHIPS = 16
HEADS = 16
COLS = HEADS * MP
TILES = COLS // 128
HOP = 5
NEAR = 8
FAR = 12
NEG = -1e30
SCALE = math.log2(math.e) / math.sqrt(HD)


def nt_dot(a, b):
    return lax.dot_general(a, b, (((1,), (1,)), ((), ())), preferred_element_type=F32)


def tn_dot(a, b):
    return lax.dot_general(a, b, (((0,), (0,)), ((), ())), preferred_element_type=F32)


def spread(table, tile):
    rows = table.shape[0]
    lane = lax.broadcasted_iota(jnp.int32, (rows, 128), 1)
    return jnp.where(lane < MP, table[:, 2 * tile : 2 * tile + 1], table[:, 2 * tile + 1 : 2 * tile + 2])


def kernel(
    offs_ref,
    step_ref,
    rate_ref,
    skip_ref,
    gain_ref,
    x_hbm,
    gate_hbm,
    write_hbm,
    read_hbm,
    q_hbm,
    k_hbm,
    v_hbm,
    mamba_ref,
    attn_ref,
    x_ref,
    gate_ref,
    b_ref,
    c_ref,
    q_ref,
    kv_ref,
    u_ref,
    carry_ref,
    er_ref,
    base_ref,
    silu_ref,
    own_ref,
    own_send,
    part_ref,
    thr_own,
    thr_part,
    comb_ref,
    comb_thr,
    in1_ref,
    thr1_ref,
    pre_ref,
    in2_ref,
    state_ref,
    other_ref,
    start_ref,
    qpos_ref,
    top_ref,
    acc_ref,
    gated_ref,
    load_sem,
    near_recv,
    pair_recv,
    near_send,
    pair_send,
    ex_send,
    ex_recv,
    s1_send,
    s1_recv,
    t1_send,
    t1_recv,
    s2_send,
    s2_recv,
):
    me = lax.axis_index("ctx")
    z, core = lax.div(me, 2), lax.rem(me, 2)
    partner = me + 1 - 2 * core
    anchor = me * TOK

    def chip(index):
        return {"ctx": 2 * index + core}

    def remote(src, dst, send, recv, device):
        return pltpu.make_async_remote_copy(
            src_ref=src, dst_ref=dst, send_sem=send, recv_sem=recv, device_id=device, device_id_type=MESH
        )

    def peer(k):
        turn = lax.div(k + 1, 2)
        away = CHIPS // 2 + jnp.where(lax.rem(k, 2) == 1, turn, -turn)
        return lax.rem(z + away, CHIPS)

    barrier = pltpu.get_barrier_semaphore()

    def greet(k, _):
        pl.semaphore_signal(barrier, inc=1, device_id=chip(peer(k)), device_id_type=MESH)
        return 0

    lax.fori_loop(0, CHIPS - 1, greet, 0)
    pl.semaphore_signal(barrier, inc=1, device_id={"ctx": partner}, device_id_type=MESH)

    loads = [
        pltpu.make_async_copy(src, dst, load_sem.at[n])
        for n, (src, dst) in enumerate(
            (
                (k_hbm, kv_ref.at[0, core, 0]),
                (v_hbm, kv_ref.at[0, core, 1]),
                (write_hbm, b_ref),
                (read_hbm, c_ref),
                (x_hbm, x_ref),
                (q_hbm, q_ref),
                (gate_hbm, gate_ref),
            )
        )
    ]
    for load in loads:
        load.start()

    row = lax.broadcasted_iota(jnp.int32, (TOK, 128), 0)
    col = lax.broadcasted_iota(jnp.int32, (TOK, 128), 1)
    pos = anchor + row
    start = jnp.zeros((TOK, 128), jnp.int32)
    final = jnp.zeros((8, 128), jnp.int32)
    for d in range(1, 32):
        off = offs_ref[d]
        start = jnp.where(pos >= off, off, start)
        final = jnp.where(anchor + TOK - 1 + jnp.zeros((8, 128), jnp.int32) >= off, off, final)
    final = final[0:1]
    start_ref[...] = start
    qpos_ref[...] = pos

    sums = jnp.concatenate([(col <= row).astype(F32), (col == row).astype(F32)], axis=0)
    sums = lax.dot_general(
        sums, step_ref[...], (((1,), (1,)), ((), ())), precision=HIGHEST, preferred_element_type=F32
    )
    running = -rate_ref[...] * sums[0:TOK]
    grow = jnp.exp(-running) * sums[TOK : 2 * TOK]
    er = jnp.exp(running)
    last = jnp.exp(running[TOK - 1 : TOK])

    for load in loads[:5]:
        load.wait()
    held = jnp.where(pos >= final, b_ref[...].astype(F32), 0.0)
    held_t = held.T.astype(BF16)
    inner = jnp.where((col <= row) & (anchor + col >= start), nt_dot(c_ref[...], b_ref[...]), 0.0)
    entering = jnp.where(start < anchor, c_ref[...].astype(F32), 0.0)
    inner = inner.astype(BF16)
    carry_ref[...] = entering.astype(BF16)
    for t in range(TILES):
        sl = slice(128 * t, 128 * t + 128)
        u = (x_ref[:, sl].astype(F32) * spread(grow, t)).astype(BF16)
        u_ref[:, sl] = u
        decay = spread(last, t)
        tile = jnp.dot(held_t, u, preferred_element_type=F32) * decay
        own_ref[4 * t : 4 * t + 4] = tile.reshape(4, 32, 128)
        own_send[4 * t : 4 * t + 4] = tile.astype(BF16).reshape(4, 32, 128)
        thr_own[t] = jnp.where(final < anchor, decay, 0.0)

    pl.semaphore_wait(barrier, CHIPS)

    def forward(d):
        return remote(kv_ref.at[d, core], kv_ref.at[d + 1, core], near_send.at[d], near_recv.at[d + 1], chip(z + 1))

    def backward(d):
        return remote(kv_ref.at[d, core], kv_ref.at[d - 1, core], near_send.at[d], near_recv.at[d - 1], chip(z - 1))

    def direct(target, sem):
        return remote(
            kv_ref.at[0, core], kv_ref.at[target - z, core], near_send.at[sem], near_recv.at[target - z], chip(target)
        )

    def leap():
        return direct(z + HOP, FAR + 1)

    def round_back():
        return direct(jnp.minimum(z + FAR, CHIPS - 1), FAR + 2)

    def pair(d):
        return remote(kv_ref.at[d, core], kv_ref.at[d, core], pair_send.at[d], pair_recv.at[d], {"ctx": partner})

    @pl.when(z < CHIPS - 1)
    def _():
        forward(0).start()

    pair(0).start()

    ex_state = remote(
        own_send.at[pl.ds(16 * (1 - core), 16)], part_ref, ex_send.at[0], ex_recv.at[0], {"ctx": partner}
    )
    ex_thr = remote(thr_own, thr_part, ex_send.at[1], ex_recv.at[1], {"ctx": partner})
    ex_state.start()
    ex_thr.start()
    ex_thr.wait_recv()
    ex_state.wait_recv()
    is_first = core == 0
    for t in range(4):
        own = own_ref[pl.ds(16 * core + 4 * t, 4)]
        part = part_ref[4 * t : 4 * t + 4].astype(F32)
        mine, theirs = thr_own[4 * core + t], thr_part[4 * core + t]
        early, late = jnp.where(is_first, own, part), jnp.where(is_first, part, own)
        comb = jnp.where(is_first, theirs, mine)[None] * early + late
        comb_ref[4 * t : 4 * t + 4] = comb.astype(BF16)
        comb_thr[4 * t : 4 * t + 4] = jnp.broadcast_to((mine * theirs)[None], (4, 1, 128))

    def s1(target, source):
        return remote(comb_ref.at[target], in1_ref.at[source], s1_send.at[target], s1_recv.at[source], chip(target))

    def t1(target, source):
        return remote(comb_thr.at[target], thr1_ref.at[source], t1_send.at[target], t1_recv.at[source], chip(target))

    def s2(target, source):
        return remote(pre_ref.at[target], in2_ref.at[source], s2_send.at[target], s2_recv.at[source], chip(target))

    def send1(k, _):
        s1(peer(k), z).start()
        t1(peer(k), z).start()
        return 0

    lax.fori_loop(0, CHIPS - 1, send1, 0)

    @pl.when(z + HOP < CHIPS)
    def _():
        leap().start()

    @pl.when(z + NEAR < CHIPS - 1)
    def _():
        round_back().start()

    in1_ref[z] = comb_ref[z]
    thr1_ref[z] = comb_thr[z]

    for load in loads[5:]:
        load.wait()
    top_ref[...] = jnp.full(top_ref.shape, NEG, F32)
    acc_ref[...] = jnp.zeros(acc_ref.shape, F32)
    heads = q_ref.shape[1] // HD

    def attend(d, causal):
        keys = jnp.concatenate([kv_ref[d, 0, 0], kv_ref[d, 1, 0]], axis=0)
        values = jnp.concatenate([kv_ref[d, 0, 1], kv_ref[d, 1, 1]], axis=0)
        values = jnp.concatenate([values, jnp.ones((2 * TOK, 128), BF16)], axis=1)
        lane = (z - d) * (2 * TOK) + lax.broadcasted_iota(jnp.int32, (TOK, 2 * TOK), 1)
        begin = start_ref[...]
        seen = lane >= jnp.concatenate([begin, begin], axis=1)
        if causal:
            here = qpos_ref[...]
            seen = seen & (lane <= jnp.concatenate([here, here], axis=1))
        for h in range(heads):
            scores = nt_dot(q_ref[:, h * HD : (h + 1) * HD], keys) * SCALE
            scores = jnp.where(seen, scores, NEG)
            before = top_ref[h]
            top = jnp.maximum(before, jnp.max(scores, axis=1, keepdims=True))
            top_ref[h] = top
            fade = jnp.exp2(before - top)
            weights = jnp.exp2(scores - jnp.concatenate([top, top], axis=1)).astype(BF16)
            update = jnp.dot(weights, values, preferred_element_type=F32)
            acc_ref[h] = acc_ref[h] * jnp.concatenate([fade, fade], axis=1) + update

    pair(0).wait_recv()
    attend(0, True)

    skip = skip_ref[...]
    for t in range(TILES):
        sl = slice(128 * t, 128 * t + 128)
        decay = spread(er, t)
        er_ref[t] = decay
        base_ref[t] = jnp.dot(inner, u_ref[:, sl], preferred_element_type=F32) * decay + spread(skip, t) * x_ref[
            :, sl
        ].astype(F32)
        gate = gate_ref[:, sl].astype(F32)
        silu_ref[t] = gate / (1.0 + jnp.exp(-gate))

    def scan():
        def arrive(k, _):
            s1(z, peer(k)).wait_recv()
            t1(z, peer(k)).wait_recv()
            return 0

        lax.fori_loop(0, CHIPS - 1, arrive, 0)
        prefix = jnp.zeros((32, 128), F32)
        for j in range(CHIPS):
            pre_ref[j] = prefix.astype(BF16)
            prefix = thr1_ref[j] * prefix + in1_ref[j].astype(F32)

        def send2(k, _):
            s2(peer(k), z).start()
            return 0

        lax.fori_loop(0, CHIPS - 1, send2, 0)
        in2_ref[z] = pre_ref[z]

    def block(d):
        pair(d).wait_recv()
        attend(d, False)

    def near_arrive(d):
        @pl.when(z >= d)
        def _():
            remote(kv_ref.at[d, core], kv_ref.at[d, core], near_send.at[d], near_recv.at[d], chip(z - d)).wait_recv()

            @pl.when((d < NEAR) & (d != HOP - 1) & (z < CHIPS - 1))
            def _():
                forward(d).start()

            @pl.when(d > NEAR + 1)
            def _():
                backward(d).start()

            pair(d).start()

    def step(n, _):
        @pl.when(n < HOP)
        def _():
            near_arrive(n)

        @pl.when(n == 1)
        def _():
            scan()

        @pl.when(n + HOP - 1 <= NEAR)
        def _():
            near_arrive(n + HOP - 1)

        @pl.when(FAR + 1 - n > NEAR)
        def _():
            near_arrive(FAR + 1 - n)

        def late(i, _):
            e = jnp.where(i == 0, n - 1, jnp.where(i == 1, n + HOP - 2, FAR + 2 - n))
            inside = jnp.where(i == 0, e < HOP, jnp.where(i == 1, e <= NEAR, e > NEAR))

            @pl.when(inside & (z >= e))
            def _():
                block(e)

            return 0

        @pl.when(n > 1)
        def _():
            lax.fori_loop(0, 3, late, 0)

        return 0

    lax.fori_loop(1, FAR - NEAR + 2, step, 0)

    def arrive2(k, _):
        s2(z, peer(k)).wait_recv()
        return 0

    lax.fori_loop(0, CHIPS - 1, arrive2, 0)
    for t in range(4):
        own = own_ref[pl.ds(16 * core + 4 * t, 4)]
        part = part_ref[4 * t : 4 * t + 4].astype(F32)
        mine, theirs = thr_own[4 * core + t], thr_part[4 * core + t]
        chip_in = in2_ref[4 * t : 4 * t + 4].astype(F32)
        second = jnp.where(is_first, mine, theirs)[None] * chip_in + jnp.where(is_first, own, part)
        state_ref[pl.ds(16 * core + 4 * t, 4)] = jnp.where(is_first, chip_in, second).astype(BF16)
        other_ref[4 * t : 4 * t + 4] = jnp.where(is_first, second, chip_in).astype(BF16)
    half = pl.ds(16 * core, 16)
    theirs_half = pl.ds(16 * (1 - core), 16)
    ex_back = remote(other_ref, state_ref.at[half], ex_send.at[2], ex_recv.at[2], {"ctx": partner})
    ex_back.start()
    for h in range(heads):
        attn_ref[:, h * HD : (h + 1) * HD] = (acc_ref[h, :, 0:HD] / acc_ref[h, :, HD : 2 * HD]).astype(BF16)

    def finish(side, square):
        for t in range(4):
            tile = 4 * side + t
            state = state_ref[pl.ds(4 * tile, 4)].reshape(128, 128)
            mixed = base_ref[tile] + er_ref[tile] * jnp.dot(carry_ref[...], state, preferred_element_type=F32)
            gated = mixed * silu_ref[tile]
            gated_ref[tile] = gated
            square = square + gated * gated
        return square

    square = finish(core, jnp.zeros((TOK, 128), F32))
    remote(other_ref, state_ref.at[theirs_half], ex_send.at[2], ex_recv.at[2], {"ctx": partner}).wait_recv()
    square = finish(1 - core, square)
    norm = lax.rsqrt(jnp.sum(square, axis=1, keepdims=True) * (1.0 / COLS) + 1e-05)
    for t in range(TILES):
        sl = slice(128 * t, 128 * t + 128)
        mamba_ref[:, sl] = (gated_ref[t] * norm * gain_ref[:, sl]).astype(BF16)

    ex_state.wait_send()
    ex_thr.wait_send()
    ex_back.wait_send()

    def sent(k, _):
        s1(peer(k), z).wait_send()
        t1(peer(k), z).wait_send()
        s2(peer(k), z).wait_send()
        return 0

    lax.fori_loop(0, CHIPS - 1, sent, 0)

    @pl.when(z + HOP < CHIPS)
    def _():
        leap().wait_send()

    @pl.when(z + NEAR < CHIPS - 1)
    def _():
        round_back().wait_send()

    def relayed(d, _):
        @pl.when(z >= d)
        def _():
            @pl.when((d < NEAR) & (d != HOP - 1) & (z < CHIPS - 1))
            def _():
                forward(d).wait_send()

            @pl.when(d > NEAR + 1)
            def _():
                backward(d).wait_send()

            pair(d).wait_send()

        return 0

    lax.fori_loop(0, FAR + 1, relayed, 0)


def per_device(
    mamba_input,
    mamba_gate,
    state_write,
    state_read,
    step_size,
    decay_rate,
    skip_scale,
    norm_gain,
    query_rows,
    key_rows,
    value_rows,
    doc_offsets,
):
    vmem, hbm = pl.BlockSpec(memory_space=pltpu.VMEM), pl.BlockSpec(memory_space=pl.ANY)
    dma = pltpu.SemaphoreType.DMA
    heads = query_rows.shape[1] // HD
    return pl.pallas_call(
        kernel,
        out_shape=(
            jax.ShapeDtypeStruct(mamba_input.shape, BF16),
            jax.ShapeDtypeStruct(query_rows.shape, BF16),
        ),
        in_specs=[pl.BlockSpec(memory_space=pltpu.SMEM)] + [vmem] * 4 + [hbm] * 7,
        out_specs=(vmem, vmem),
        scratch_shapes=[
            pltpu.VMEM((TOK, COLS), BF16),
            pltpu.VMEM((TOK, COLS), BF16),
            pltpu.VMEM((TOK, 128), BF16),
            pltpu.VMEM((TOK, 128), BF16),
            pltpu.VMEM((TOK, heads * HD), BF16),
            pltpu.VMEM((FAR + 1, 2, 2, TOK, HD), BF16),
            pltpu.VMEM((TOK, COLS), BF16),
            pltpu.VMEM((TOK, 128), BF16),
            pltpu.VMEM((TILES, TOK, 128), F32),
            pltpu.VMEM((TILES, TOK, 128), F32),
            pltpu.VMEM((TILES, TOK, 128), F32),
            pltpu.VMEM((32, 32, 128), F32),
            pltpu.VMEM((32, 32, 128), BF16),
            pltpu.VMEM((16, 32, 128), BF16),
            pltpu.VMEM((TILES, 1, 128), F32),
            pltpu.VMEM((TILES, 1, 128), F32),
            pltpu.VMEM((CHIPS, 32, 128), BF16),
            pltpu.VMEM((CHIPS, 1, 128), F32),
            pltpu.VMEM((CHIPS, 32, 128), BF16),
            pltpu.VMEM((CHIPS, 1, 128), F32),
            pltpu.VMEM((CHIPS, 32, 128), BF16),
            pltpu.VMEM((CHIPS, 32, 128), BF16),
            pltpu.VMEM((32, 32, 128), BF16),
            pltpu.VMEM((16, 32, 128), BF16),
            pltpu.VMEM((TOK, 128), jnp.int32),
            pltpu.VMEM((TOK, 128), jnp.int32),
            pltpu.VMEM((heads, TOK, 128), F32),
            pltpu.VMEM((heads, TOK, 256), F32),
            pltpu.VMEM((TILES, TOK, 128), F32),
            dma((7,)),
            dma((FAR + 1,)),
            dma((FAR + 1,)),
            dma((FAR + 3,)),
            dma((FAR + 1,)),
            dma((3,)),
            dma((3,)),
            dma((CHIPS,)),
            dma((CHIPS,)),
            dma((CHIPS,)),
            dma((CHIPS,)),
            dma((CHIPS,)),
            dma((CHIPS,)),
        ],
        compiler_params=pltpu.CompilerParams(collective_id=0, has_side_effects=True),
    )(
        doc_offsets,
        step_size.T,
        decay_rate.reshape(1, -1),
        skip_scale.reshape(1, -1),
        norm_gain.reshape(1, -1),
        mamba_input,
        mamba_gate,
        state_write,
        state_read,
        query_rows,
        key_rows,
        value_rows,
    )


def solution(mesh):
    rows, cols = P(("dp", "ctx"), "tensor"), P("tensor")
    return jax.shard_map(
        per_device,
        mesh=mesh,
        in_specs=(rows,) * 5 + (cols,) * 3 + (rows,) * 3 + (P("dp"),),
        out_specs=(rows, rows),
        check_vma=False,
    )
```

```python
import functools
import math

import jax
import jax.numpy as jnp
from jax import lax
from jax.experimental import pallas as pl
from jax.experimental.pallas import tpu as pltpu
from jax.sharding import PartitionSpec as P

MESH = pl.DeviceIdType.MESH
HIGHEST = lax.Precision.HIGHEST
F32, BF16 = jnp.float32, jnp.bfloat16

MP = 64
HD = 128
TOK = 128
CHIPS = 16
HEADS = 16
COLS = HEADS * MP
TILES = COLS // 128
HOP = 5
NEAR = 9
FAR = 12
STEPS = max(HOP - 1, NEAR - HOP + 1, FAR - NEAR) + 1
NEG = -1e30
SCALE = math.log2(math.e) / math.sqrt(HD)


def nt_dot(a, b):
    return lax.dot_general(a, b, (((1,), (1,)), ((), ())), preferred_element_type=F32)


def tn_dot(a, b):
    return lax.dot_general(a, b, (((0,), (0,)), ((), ())), preferred_element_type=F32)


def spread(table, tile):
    rows = table.shape[0]
    lane = lax.broadcasted_iota(jnp.int32, (rows, 128), 1)
    return jnp.where(lane < MP, table[:, 2 * tile : 2 * tile + 1], table[:, 2 * tile + 1 : 2 * tile + 2])


def kernel(
    offs_ref,
    step_ref,
    rate_ref,
    skip_ref,
    gain_ref,
    x_hbm,
    gate_hbm,
    write_hbm,
    read_hbm,
    q_hbm,
    k_hbm,
    v_hbm,
    mamba_ref,
    attn_ref,
    x_ref,
    gate_ref,
    b_ref,
    c_ref,
    q_ref,
    kv_ref,
    u_ref,
    carry_ref,
    er_ref,
    base_ref,
    silu_ref,
    own_ref,
    own_send,
    part_ref,
    thr_own,
    thr_part,
    comb_ref,
    comb_thr,
    in1_ref,
    thr1_ref,
    pre_ref,
    in2_ref,
    state_ref,
    other_ref,
    start_ref,
    qpos_ref,
    top_ref,
    acc_ref,
    gated_ref,
    load_sem,
    near_recv,
    pair_recv,
    near_send,
    pair_send,
    ex_send,
    ex_recv,
    s1_send,
    s1_recv,
    t1_send,
    t1_recv,
    s2_send,
    s2_recv,
):
    me = lax.axis_index("ctx")
    z, core = lax.div(me, 2), lax.rem(me, 2)
    partner = me + 1 - 2 * core
    anchor = me * TOK

    def chip(index):
        return {"ctx": 2 * index + core}

    def remote(src, dst, send, recv, device):
        return pltpu.make_async_remote_copy(
            src_ref=src, dst_ref=dst, send_sem=send, recv_sem=recv, device_id=device, device_id_type=MESH
        )

    def peer(k):
        turn = lax.div(k + 1, 2)
        away = CHIPS // 2 + jnp.where(lax.rem(k, 2) == 1, turn, -turn)
        return lax.rem(z + away, CHIPS)

    barrier = pltpu.get_barrier_semaphore()

    def greet(k, _):
        pl.semaphore_signal(barrier, inc=1, device_id=chip(peer(k)), device_id_type=MESH)
        return 0

    lax.fori_loop(0, CHIPS - 1, greet, 0)
    pl.semaphore_signal(barrier, inc=1, device_id={"ctx": partner}, device_id_type=MESH)

    loads = [
        pltpu.make_async_copy(src, dst, load_sem.at[n])
        for n, (src, dst) in enumerate(
            (
                (write_hbm, b_ref),
                (x_hbm, x_ref),
                (k_hbm, kv_ref.at[0, core, 0]),
                (v_hbm, kv_ref.at[0, core, 1]),
                (read_hbm, c_ref),
                (q_hbm, q_ref),
                (gate_hbm, gate_ref),
            )
        )
    ]
    for load in loads:
        load.start()

    row = lax.broadcasted_iota(jnp.int32, (TOK, 128), 0)
    col = lax.broadcasted_iota(jnp.int32, (TOK, 128), 1)
    pos = anchor + row
    start = jnp.zeros((TOK, 128), jnp.int32)
    final = jnp.zeros((8, 128), jnp.int32)
    for d in range(1, 32):
        off = offs_ref[d]
        start = jnp.where(pos >= off, off, start)
        final = jnp.where(anchor + TOK - 1 + jnp.zeros((8, 128), jnp.int32) >= off, off, final)
    final = final[0:1]
    start_ref[...] = start
    qpos_ref[...] = pos

    sums = jnp.concatenate([(col <= row).astype(F32), (col == row).astype(F32)], axis=0)
    sums = lax.dot_general(
        sums, step_ref[...], (((1,), (1,)), ((), ())), precision=HIGHEST, preferred_element_type=F32
    )
    running = -rate_ref[...] * sums[0:TOK]
    grow = jnp.exp(-running) * sums[TOK : 2 * TOK]
    er = jnp.exp(running)
    last = jnp.exp(running[TOK - 1 : TOK])

    for load in loads[:2]:
        load.wait()
    held = jnp.where(pos >= final, b_ref[...].astype(F32), 0.0)
    held_t = held.T.astype(BF16)
    for t in range(TILES):
        sl = slice(128 * t, 128 * t + 128)
        u = (x_ref[:, sl].astype(F32) * spread(grow, t)).astype(BF16)
        u_ref[:, sl] = u
        decay = spread(last, t)
        tile = jnp.dot(held_t, u, preferred_element_type=F32) * decay
        own_ref[4 * t : 4 * t + 4] = tile.reshape(4, 32, 128)
        own_send[4 * t : 4 * t + 4] = tile.astype(BF16).reshape(4, 32, 128)
        thr_own[t] = jnp.where(final < anchor, decay, 0.0)

    for load in loads[2:4]:
        load.wait()
    pl.semaphore_wait(barrier, CHIPS)

    def hop(d, e, part, sem, device):
        return remote(
            kv_ref.at[d, core, part], kv_ref.at[e, core, part], near_send.at[sem, part], near_recv.at[e, part], device
        )

    def forward(d, part):
        return hop(d, d + 1, part, d, chip(z + 1))

    def backward(d, part):
        return hop(d, d - 1, part, d, chip(z - 1))

    def leap(part):
        return hop(0, HOP, part, FAR + 1, chip(z + HOP))

    def round_back(part):
        target = jnp.minimum(z + FAR, CHIPS - 1)
        return hop(0, target - z, part, FAR + 2, chip(target))

    def pair(d):
        return remote(kv_ref.at[d, core], kv_ref.at[d, core], pair_send.at[d], pair_recv.at[d], {"ctx": partner})

    @pl.when(z < CHIPS - 1)
    def _():
        forward(0, 0).start()
        forward(0, 1).start()

    pair(0).start()

    ex_state = remote(
        own_send.at[pl.ds(16 * (1 - core), 16)], part_ref, ex_send.at[0], ex_recv.at[0], {"ctx": partner}
    )
    ex_thr = remote(thr_own, thr_part, ex_send.at[1], ex_recv.at[1], {"ctx": partner})
    ex_state.start()
    ex_thr.start()
    ex_thr.wait_recv()
    ex_state.wait_recv()
    is_first = core == 0
    for t in range(4):
        own = own_ref[pl.ds(16 * core + 4 * t, 4)]
        part = part_ref[4 * t : 4 * t + 4].astype(F32)
        mine, theirs = thr_own[4 * core + t], thr_part[4 * core + t]
        early, late = jnp.where(is_first, own, part), jnp.where(is_first, part, own)
        comb = jnp.where(is_first, theirs, mine)[None] * early + late
        comb_ref[4 * t : 4 * t + 4] = comb.astype(BF16)
        comb_thr[4 * t : 4 * t + 4] = jnp.broadcast_to((mine * theirs)[None], (4, 1, 128))

    def s1(target, source):
        return remote(comb_ref.at[target], in1_ref.at[source], s1_send.at[target], s1_recv.at[source], chip(target))

    def t1(target, source):
        return remote(comb_thr.at[target], thr1_ref.at[source], t1_send.at[target], t1_recv.at[source], chip(target))

    def s2(target, source):
        return remote(pre_ref.at[target], in2_ref.at[source], s2_send.at[target], s2_recv.at[source], chip(target))

    def send1(k, _):
        s1(peer(k), z).start()
        t1(peer(k), z).start()
        return 0

    lax.fori_loop(0, CHIPS - 1, send1, 0)

    @pl.when(z + HOP < CHIPS)
    def _():
        leap(0).start()
        leap(1).start()

    @pl.when(z + NEAR < CHIPS - 1)
    def _():
        round_back(0).start()
        round_back(1).start()

    in1_ref[z] = comb_ref[z]
    thr1_ref[z] = comb_thr[z]

    for load in loads[4:]:
        load.wait()
    top_ref[...] = jnp.full(top_ref.shape, NEG, F32)
    acc_ref[...] = jnp.zeros(acc_ref.shape, F32)
    heads = q_ref.shape[1] // HD

    def attend(d, causal):
        keys = jnp.concatenate([kv_ref[d, 0, 0], kv_ref[d, 1, 0]], axis=0)
        values = jnp.concatenate([kv_ref[d, 0, 1], kv_ref[d, 1, 1]], axis=0)
        values = jnp.concatenate([values, jnp.ones((2 * TOK, 128), BF16)], axis=1)
        lane = (z - d) * (2 * TOK) + lax.broadcasted_iota(jnp.int32, (TOK, 2 * TOK), 1)
        begin = start_ref[...]
        seen = lane >= jnp.concatenate([begin, begin], axis=1)
        if causal:
            here = qpos_ref[...]
            seen = seen & (lane <= jnp.concatenate([here, here], axis=1))
        for h in range(heads):
            scores = nt_dot(q_ref[:, h * HD : (h + 1) * HD], keys) * SCALE
            scores = jnp.where(seen, scores, NEG)
            before = top_ref[h]
            top = jnp.maximum(before, jnp.max(scores, axis=1, keepdims=True))
            top_ref[h] = top
            fade = jnp.exp2(before - top)
            weights = jnp.exp2(scores - jnp.concatenate([top, top], axis=1)).astype(BF16)
            update = jnp.dot(weights, values, preferred_element_type=F32)
            acc_ref[h] = acc_ref[h] * jnp.concatenate([fade, fade], axis=1) + update

    pair(0).wait_recv()
    attend(0, True)

    inner = jnp.where((col <= row) & (anchor + col >= start), nt_dot(c_ref[...], b_ref[...]), 0.0).astype(BF16)
    carry_ref[...] = jnp.where(start < anchor, c_ref[...].astype(F32), 0.0).astype(BF16)
    skip = skip_ref[...]
    for t in range(TILES):
        sl = slice(128 * t, 128 * t + 128)
        decay = spread(er, t)
        er_ref[t] = decay
        base_ref[t] = jnp.dot(inner, u_ref[:, sl], preferred_element_type=F32) * decay + spread(skip, t) * x_ref[
            :, sl
        ].astype(F32)
        gate = gate_ref[:, sl].astype(F32)
        silu_ref[t] = gate / (1.0 + jnp.exp(-gate))

    def scan():
        def arrive(k, _):
            s1(z, peer(k)).wait_recv()
            t1(z, peer(k)).wait_recv()
            return 0

        lax.fori_loop(0, CHIPS - 1, arrive, 0)
        prefix = jnp.zeros((32, 128), F32)
        for j in range(CHIPS):
            pre_ref[j] = prefix.astype(BF16)
            prefix = thr1_ref[j] * prefix + in1_ref[j].astype(F32)

        def send2(k, _):
            s2(peer(k), z).start()
            return 0

        lax.fori_loop(0, CHIPS - 1, send2, 0)
        in2_ref[z] = pre_ref[z]

    def block(d):
        pair(d).wait_recv()
        attend(d, False)

    def near_arrive(d):
        @pl.when(z >= d)
        def _():
            for part in range(2):
                hop(d, d, part, d, chip(z - d)).wait_recv()

                @pl.when((d < NEAR) & (d != HOP - 1) & (z < CHIPS - 1))
                def _(part=part):
                    forward(d, part).start()

                @pl.when(d > NEAR + 1)
                def _(part=part):
                    backward(d, part).start()

            pair(d).start()

    def step(n, _):
        @pl.when(n < HOP)
        def _():
            near_arrive(n)

        @pl.when(n == 1)
        def _():
            scan()

        @pl.when(n + HOP - 1 <= NEAR)
        def _():
            near_arrive(n + HOP - 1)

        @pl.when(FAR + 1 - n > NEAR)
        def _():
            near_arrive(FAR + 1 - n)

        def late(i, _):
            e = jnp.where(i == 0, n - 1, jnp.where(i == 1, n + HOP - 2, FAR + 2 - n))
            inside = jnp.where(i == 0, e < HOP, jnp.where(i == 1, e <= NEAR, e > NEAR))

            @pl.when(inside & (z >= e))
            def _():
                block(e)

            return 0

        @pl.when(n > 1)
        def _():
            lax.fori_loop(0, 3, late, 0)

        return 0

    lax.fori_loop(1, STEPS + 1, step, 0)

    def arrive2(k, _):
        s2(z, peer(k)).wait_recv()
        return 0

    lax.fori_loop(0, CHIPS - 1, arrive2, 0)
    for t in range(4):
        own = own_ref[pl.ds(16 * core + 4 * t, 4)]
        part = part_ref[4 * t : 4 * t + 4].astype(F32)
        mine, theirs = thr_own[4 * core + t], thr_part[4 * core + t]
        chip_in = in2_ref[4 * t : 4 * t + 4].astype(F32)
        second = jnp.where(is_first, mine, theirs)[None] * chip_in + jnp.where(is_first, own, part)
        state_ref[pl.ds(16 * core + 4 * t, 4)] = jnp.where(is_first, chip_in, second).astype(BF16)
        other_ref[4 * t : 4 * t + 4] = jnp.where(is_first, second, chip_in).astype(BF16)
    half = pl.ds(16 * core, 16)
    theirs_half = pl.ds(16 * (1 - core), 16)
    ex_back = remote(other_ref, state_ref.at[half], ex_send.at[2], ex_recv.at[2], {"ctx": partner})
    ex_back.start()
    for h in range(heads):
        attn_ref[:, h * HD : (h + 1) * HD] = (acc_ref[h, :, 0:HD] / acc_ref[h, :, HD : 2 * HD]).astype(BF16)

    def finish(side, square):
        for t in range(4):
            tile = 4 * side + t
            state = state_ref[pl.ds(4 * tile, 4)].reshape(128, 128)
            mixed = base_ref[tile] + er_ref[tile] * jnp.dot(carry_ref[...], state, preferred_element_type=F32)
            gated = mixed * silu_ref[tile]
            gated_ref[tile] = gated
            square = square + gated * gated
        return square

    square = finish(core, jnp.zeros((TOK, 128), F32))
    remote(other_ref, state_ref.at[theirs_half], ex_send.at[2], ex_recv.at[2], {"ctx": partner}).wait_recv()
    square = finish(1 - core, square)
    norm = lax.rsqrt(jnp.sum(square, axis=1, keepdims=True) * (1.0 / COLS) + 1e-05)
    for t in range(TILES):
        sl = slice(128 * t, 128 * t + 128)
        mamba_ref[:, sl] = (gated_ref[t] * norm * gain_ref[:, sl]).astype(BF16)

    ex_state.wait_send()
    ex_thr.wait_send()
    ex_back.wait_send()

    def sent(k, _):
        s1(peer(k), z).wait_send()
        t1(peer(k), z).wait_send()
        s2(peer(k), z).wait_send()
        return 0

    lax.fori_loop(0, CHIPS - 1, sent, 0)

    @pl.when(z + HOP < CHIPS)
    def _():
        leap(0).wait_send()
        leap(1).wait_send()

    @pl.when(z + NEAR < CHIPS - 1)
    def _():
        round_back(0).wait_send()
        round_back(1).wait_send()

    def relayed(d, _):
        @pl.when(z >= d)
        def _():
            @pl.when((d < NEAR) & (d != HOP - 1) & (z < CHIPS - 1))
            def _():
                forward(d, 0).wait_send()
                forward(d, 1).wait_send()

            @pl.when(d > NEAR + 1)
            def _():
                backward(d, 0).wait_send()
                backward(d, 1).wait_send()

            pair(d).wait_send()

        return 0

    lax.fori_loop(0, FAR + 1, relayed, 0)


def per_device(
    mamba_input,
    mamba_gate,
    state_write,
    state_read,
    step_size,
    decay_rate,
    skip_scale,
    norm_gain,
    query_rows,
    key_rows,
    value_rows,
    doc_offsets,
):
    vmem, hbm = pl.BlockSpec(memory_space=pltpu.VMEM), pl.BlockSpec(memory_space=pl.ANY)
    dma = pltpu.SemaphoreType.DMA
    heads = query_rows.shape[1] // HD
    return pl.pallas_call(
        kernel,
        out_shape=(
            jax.ShapeDtypeStruct(mamba_input.shape, BF16),
            jax.ShapeDtypeStruct(query_rows.shape, BF16),
        ),
        in_specs=[pl.BlockSpec(memory_space=pltpu.SMEM)] + [vmem] * 4 + [hbm] * 7,
        out_specs=(vmem, vmem),
        scratch_shapes=[
            pltpu.VMEM((TOK, COLS), BF16),
            pltpu.VMEM((TOK, COLS), BF16),
            pltpu.VMEM((TOK, 128), BF16),
            pltpu.VMEM((TOK, 128), BF16),
            pltpu.VMEM((TOK, heads * HD), BF16),
            pltpu.VMEM((FAR + 1, 2, 2, TOK, HD), BF16),
            pltpu.VMEM((TOK, COLS), BF16),
            pltpu.VMEM((TOK, 128), BF16),
            pltpu.VMEM((TILES, TOK, 128), F32),
            pltpu.VMEM((TILES, TOK, 128), F32),
            pltpu.VMEM((TILES, TOK, 128), F32),
            pltpu.VMEM((32, 32, 128), F32),
            pltpu.VMEM((32, 32, 128), BF16),
            pltpu.VMEM((16, 32, 128), BF16),
            pltpu.VMEM((TILES, 1, 128), F32),
            pltpu.VMEM((TILES, 1, 128), F32),
            pltpu.VMEM((CHIPS, 32, 128), BF16),
            pltpu.VMEM((CHIPS, 1, 128), F32),
            pltpu.VMEM((CHIPS, 32, 128), BF16),
            pltpu.VMEM((CHIPS, 1, 128), F32),
            pltpu.VMEM((CHIPS, 32, 128), BF16),
            pltpu.VMEM((CHIPS, 32, 128), BF16),
            pltpu.VMEM((32, 32, 128), BF16),
            pltpu.VMEM((16, 32, 128), BF16),
            pltpu.VMEM((TOK, 128), jnp.int32),
            pltpu.VMEM((TOK, 128), jnp.int32),
            pltpu.VMEM((heads, TOK, 128), F32),
            pltpu.VMEM((heads, TOK, 256), F32),
            pltpu.VMEM((TILES, TOK, 128), F32),
            dma((7,)),
            dma((FAR + 1, 2)),
            dma((FAR + 1,)),
            dma((FAR + 3, 2)),
            dma((FAR + 1,)),
            dma((3,)),
            dma((3,)),
            dma((CHIPS,)),
            dma((CHIPS,)),
            dma((CHIPS,)),
            dma((CHIPS,)),
            dma((CHIPS,)),
            dma((CHIPS,)),
        ],
        compiler_params=pltpu.CompilerParams(collective_id=0, has_side_effects=True),
    )(
        doc_offsets,
        step_size.T,
        decay_rate.reshape(1, -1),
        skip_scale.reshape(1, -1),
        norm_gain.reshape(1, -1),
        mamba_input,
        mamba_gate,
        state_write,
        state_read,
        query_rows,
        key_rows,
        value_rows,
    )


def solution(mesh):
    rows, cols = P(("dp", "ctx"), "tensor"), P("tensor")
    return jax.shard_map(
        per_device,
        mesh=mesh,
        in_specs=(rows,) * 5 + (cols,) * 3 + (rows,) * 3 + (P("dp"),),
        out_specs=(rows, rows),
        check_vma=False,
    )
```

```python
import functools
import math

import jax
import jax.numpy as jnp
from jax import lax
from jax.experimental import pallas as pl
from jax.experimental.pallas import tpu as pltpu
from jax.sharding import PartitionSpec as P

MESH = pl.DeviceIdType.MESH
HIGHEST = lax.Precision.HIGHEST
F32, BF16 = jnp.float32, jnp.bfloat16

MP = 64
HD = 128
TOK = 128
CHIPS = 16
HEADS = 16
COLS = HEADS * MP
TILES = COLS // 128
HOP = 5
NEAR = 8
FAR = 12
STEPS = max(HOP - 1, NEAR - HOP + 1, FAR - NEAR) + 1
NEG = -1e30
SCALE = math.log2(math.e) / math.sqrt(HD)


def nt_dot(a, b):
    return lax.dot_general(a, b, (((1,), (1,)), ((), ())), preferred_element_type=F32)


def tn_dot(a, b):
    return lax.dot_general(a, b, (((0,), (0,)), ((), ())), preferred_element_type=F32)


def spread(table, tile):
    rows = table.shape[0]
    lane = lax.broadcasted_iota(jnp.int32, (rows, 128), 1)
    return jnp.where(lane < MP, table[:, 2 * tile : 2 * tile + 1], table[:, 2 * tile + 1 : 2 * tile + 2])


def kernel(
    offs_ref,
    step_ref,
    rate_ref,
    skip_ref,
    gain_ref,
    x_hbm,
    gate_hbm,
    write_hbm,
    read_hbm,
    q_hbm,
    k_hbm,
    v_hbm,
    mamba_ref,
    attn_ref,
    x_ref,
    gate_ref,
    b_ref,
    c_ref,
    q_ref,
    kv_ref,
    u_ref,
    carry_ref,
    er_ref,
    base_ref,
    silu_ref,
    own_ref,
    own_send,
    part_ref,
    thr_own,
    thr_part,
    comb_ref,
    comb_thr,
    in1_ref,
    thr1_ref,
    pre_ref,
    in2_ref,
    state_ref,
    other_ref,
    start_ref,
    qpos_ref,
    top_ref,
    acc_ref,
    gated_ref,
    load_sem,
    near_recv,
    pair_recv,
    near_send,
    pair_send,
    ex_send,
    ex_recv,
    s1_send,
    s1_recv,
    t1_send,
    t1_recv,
    s2_send,
    s2_recv,
):
    me = lax.axis_index("ctx")
    z, core = lax.div(me, 2), lax.rem(me, 2)
    partner = me + 1 - 2 * core
    anchor = me * TOK

    def chip(index):
        return {"ctx": 2 * index + core}

    def remote(src, dst, send, recv, device):
        return pltpu.make_async_remote_copy(
            src_ref=src, dst_ref=dst, send_sem=send, recv_sem=recv, device_id=device, device_id_type=MESH
        )

    def peer(k):
        turn = lax.div(k + 1, 2)
        away = CHIPS // 2 + jnp.where(lax.rem(k, 2) == 1, turn, -turn)
        return lax.rem(z + away, CHIPS)

    barrier = pltpu.get_barrier_semaphore()

    def greet(k, _):
        pl.semaphore_signal(barrier, inc=1, device_id=chip(peer(k)), device_id_type=MESH)
        return 0

    lax.fori_loop(0, CHIPS - 1, greet, 0)
    pl.semaphore_signal(barrier, inc=1, device_id={"ctx": partner}, device_id_type=MESH)

    loads = [
        pltpu.make_async_copy(src, dst, load_sem.at[n])
        for n, (src, dst) in enumerate(
            (
                (write_hbm, b_ref),
                (x_hbm, x_ref),
                (k_hbm, kv_ref.at[0, core, 0]),
                (v_hbm, kv_ref.at[0, core, 1]),
                (read_hbm, c_ref),
                (q_hbm, q_ref),
                (gate_hbm, gate_ref),
            )
        )
    ]
    for load in loads:
        load.start()

    row = lax.broadcasted_iota(jnp.int32, (TOK, 128), 0)
    col = lax.broadcasted_iota(jnp.int32, (TOK, 128), 1)
    pos = anchor + row
    start = jnp.zeros((TOK, 128), jnp.int32)
    final = jnp.zeros((8, 128), jnp.int32)
    for d in range(1, 32):
        off = offs_ref[d]
        start = jnp.where(pos >= off, off, start)
        final = jnp.where(anchor + TOK - 1 + jnp.zeros((8, 128), jnp.int32) >= off, off, final)
    final = final[0:1]
    start_ref[...] = start
    qpos_ref[...] = pos

    sums = jnp.concatenate([(col <= row).astype(F32), (col == row).astype(F32)], axis=0)
    sums = lax.dot_general(
        sums, step_ref[...], (((1,), (1,)), ((), ())), precision=HIGHEST, preferred_element_type=F32
    )
    running = -rate_ref[...] * sums[0:TOK]
    grow = jnp.exp(-running) * sums[TOK : 2 * TOK]
    er = jnp.exp(running)
    last = jnp.exp(running[TOK - 1 : TOK])

    for load in loads[:2]:
        load.wait()
    held = jnp.where(pos >= final, b_ref[...].astype(F32), 0.0)
    held_t = held.T.astype(BF16)
    for t in range(TILES):
        sl = slice(128 * t, 128 * t + 128)
        u = (x_ref[:, sl].astype(F32) * spread(grow, t)).astype(BF16)
        u_ref[:, sl] = u
        decay = spread(last, t)
        tile = jnp.dot(held_t, u, preferred_element_type=F32) * decay
        own_ref[4 * t : 4 * t + 4] = tile.reshape(4, 32, 128)
        own_send[4 * t : 4 * t + 4] = tile.astype(BF16).reshape(4, 32, 128)
        thr_own[t] = jnp.where(final < anchor, decay, 0.0)

    for load in loads[2:4]:
        load.wait()
    pl.semaphore_wait(barrier, CHIPS)

    def hop(d, e, part, sem, device):
        return remote(
            kv_ref.at[d, core, part], kv_ref.at[e, core, part], near_send.at[sem, part], near_recv.at[e, part], device
        )

    def forward(d, part):
        return hop(d, d + 1, part, d, chip(z + 1))

    def backward(d, part):
        return hop(d, d - 1, part, d, chip(z - 1))

    def leap(part):
        return hop(0, HOP, part, FAR + 1, chip(z + HOP))

    def round_back(part):
        target = jnp.minimum(z + FAR, CHIPS - 1)
        return hop(0, target - z, part, FAR + 2, chip(target))

    def pair(d):
        return remote(kv_ref.at[d, core], kv_ref.at[d, core], pair_send.at[d], pair_recv.at[d], {"ctx": partner})

    @pl.when(z < CHIPS - 1)
    def _():
        forward(0, 0).start()
        forward(0, 1).start()

    pair(0).start()

    ex_state = remote(
        own_send.at[pl.ds(16 * (1 - core), 16)], part_ref, ex_send.at[0], ex_recv.at[0], {"ctx": partner}
    )
    ex_thr = remote(thr_own, thr_part, ex_send.at[1], ex_recv.at[1], {"ctx": partner})
    ex_state.start()
    ex_thr.start()
    ex_thr.wait_recv()
    ex_state.wait_recv()
    is_first = core == 0
    for t in range(4):
        own = own_ref[pl.ds(16 * core + 4 * t, 4)]
        part = part_ref[4 * t : 4 * t + 4].astype(F32)
        mine, theirs = thr_own[4 * core + t], thr_part[4 * core + t]
        early, late = jnp.where(is_first, own, part), jnp.where(is_first, part, own)
        comb = jnp.where(is_first, theirs, mine)[None] * early + late
        comb_ref[4 * t : 4 * t + 4] = comb.astype(BF16)
        comb_thr[4 * t : 4 * t + 4] = jnp.broadcast_to((mine * theirs)[None], (4, 1, 128))

    def s1(target, source):
        return remote(comb_ref.at[target], in1_ref.at[source], s1_send.at[target], s1_recv.at[source], chip(target))

    def t1(target, source):
        return remote(comb_thr.at[target], thr1_ref.at[source], t1_send.at[target], t1_recv.at[source], chip(target))

    def s2(target, source):
        return remote(pre_ref.at[target], in2_ref.at[source], s2_send.at[target], s2_recv.at[source], chip(target))

    def send1(k, _):
        s1(peer(k), z).start()
        t1(peer(k), z).start()
        return 0

    lax.fori_loop(0, CHIPS - 1, send1, 0)

    @pl.when(z + HOP < CHIPS)
    def _():
        leap(0).start()
        leap(1).start()

    @pl.when(z + NEAR < CHIPS - 1)
    def _():
        round_back(0).start()
        round_back(1).start()

    in1_ref[z] = comb_ref[z]
    thr1_ref[z] = comb_thr[z]

    for load in loads[4:]:
        load.wait()
    top_ref[...] = jnp.full(top_ref.shape, NEG, F32)
    acc_ref[...] = jnp.zeros(acc_ref.shape, F32)
    heads = q_ref.shape[1] // HD

    def attend(d, causal):
        keys = jnp.concatenate([kv_ref[d, 0, 0], kv_ref[d, 1, 0]], axis=0)
        values = jnp.concatenate([kv_ref[d, 0, 1], kv_ref[d, 1, 1]], axis=0)
        values = jnp.concatenate([values, jnp.ones((2 * TOK, 128), BF16)], axis=1)
        lane = (z - d) * (2 * TOK) + lax.broadcasted_iota(jnp.int32, (TOK, 2 * TOK), 1)
        begin = start_ref[...]
        seen = lane >= jnp.concatenate([begin, begin], axis=1)
        if causal:
            here = qpos_ref[...]
            seen = seen & (lane <= jnp.concatenate([here, here], axis=1))
        for h in range(heads):
            scores = nt_dot(q_ref[:, h * HD : (h + 1) * HD], keys) * SCALE
            scores = jnp.where(seen, scores, NEG)
            before = top_ref[h]
            top = jnp.maximum(before, jnp.max(scores, axis=1, keepdims=True))
            top_ref[h] = top
            fade = jnp.exp2(before - top)
            weights = jnp.exp2(scores - jnp.concatenate([top, top], axis=1)).astype(BF16)
            update = jnp.dot(weights, values, preferred_element_type=F32)
            acc_ref[h] = acc_ref[h] * jnp.concatenate([fade, fade], axis=1) + update

    pair(0).wait_recv()
    attend(0, True)

    inner = jnp.where((col <= row) & (anchor + col >= start), nt_dot(c_ref[...], b_ref[...]), 0.0).astype(BF16)
    carry_ref[...] = jnp.where(start < anchor, c_ref[...].astype(F32), 0.0).astype(BF16)
    skip = skip_ref[...]
    for t in range(TILES):
        sl = slice(128 * t, 128 * t + 128)
        decay = spread(er, t)
        er_ref[t] = decay
        base_ref[t] = jnp.dot(inner, u_ref[:, sl], preferred_element_type=F32) * decay + spread(skip, t) * x_ref[
            :, sl
        ].astype(F32)
        gate = gate_ref[:, sl].astype(F32)
        silu_ref[t] = gate / (1.0 + jnp.exp(-gate))

    def scan():
        def arrive(k, _):
            s1(z, peer(k)).wait_recv()
            t1(z, peer(k)).wait_recv()
            return 0

        lax.fori_loop(0, CHIPS - 1, arrive, 0)
        prefix = jnp.zeros((32, 128), F32)
        for j in range(CHIPS):
            pre_ref[j] = prefix.astype(BF16)
            prefix = thr1_ref[j] * prefix + in1_ref[j].astype(F32)

        def send2(k, _):
            s2(peer(k), z).start()
            return 0

        lax.fori_loop(0, CHIPS - 1, send2, 0)
        in2_ref[z] = pre_ref[z]

    def block(d):
        pair(d).wait_recv()
        attend(d, False)

    def near_arrive(d):
        @pl.when(z >= d)
        def _():
            for part in range(2):
                hop(d, d, part, d, chip(z - d)).wait_recv()

                @pl.when((d < NEAR) & (d != HOP - 1) & (z < CHIPS - 1))
                def _(part=part):
                    forward(d, part).start()

                @pl.when(d > NEAR + 1)
                def _(part=part):
                    backward(d, part).start()

            pair(d).start()

    def step(n, _):
        @pl.when(n < HOP)
        def _():
            near_arrive(n)

        @pl.when(n == 1)
        def _():
            scan()

        @pl.when(n + HOP - 1 <= NEAR)
        def _():
            near_arrive(n + HOP - 1)

        @pl.when(FAR + 1 - n > NEAR)
        def _():
            near_arrive(FAR + 1 - n)

        def late(i, _):
            e = jnp.where(i == 0, n - 1, jnp.where(i == 1, n + HOP - 2, FAR + 2 - n))
            inside = jnp.where(i == 0, e < HOP, jnp.where(i == 1, e <= NEAR, e > NEAR))

            @pl.when(inside & (z >= e))
            def _():
                block(e)

            return 0

        @pl.when(n > 1)
        def _():
            lax.fori_loop(0, 3, late, 0)

        return 0

    lax.fori_loop(1, STEPS + 1, step, 0)

    def arrive2(k, _):
        s2(z, peer(k)).wait_recv()
        return 0

    lax.fori_loop(0, CHIPS - 1, arrive2, 0)
    for t in range(4):
        own = own_ref[pl.ds(16 * core + 4 * t, 4)]
        part = part_ref[4 * t : 4 * t + 4].astype(F32)
        mine, theirs = thr_own[4 * core + t], thr_part[4 * core + t]
        chip_in = in2_ref[4 * t : 4 * t + 4].astype(F32)
        second = jnp.where(is_first, mine, theirs)[None] * chip_in + jnp.where(is_first, own, part)
        state_ref[pl.ds(16 * core + 4 * t, 4)] = jnp.where(is_first, chip_in, second).astype(BF16)
        other_ref[4 * t : 4 * t + 4] = jnp.where(is_first, second, chip_in).astype(BF16)
    half = pl.ds(16 * core, 16)
    theirs_half = pl.ds(16 * (1 - core), 16)
    ex_back = remote(other_ref, state_ref.at[half], ex_send.at[2], ex_recv.at[2], {"ctx": partner})
    ex_back.start()
    for h in range(heads):
        attn_ref[:, h * HD : (h + 1) * HD] = (acc_ref[h, :, 0:HD] / acc_ref[h, :, HD : 2 * HD]).astype(BF16)

    def finish(side, square):
        for t in range(4):
            tile = 4 * side + t
            state = state_ref[pl.ds(4 * tile, 4)].reshape(128, 128)
            mixed = base_ref[tile] + er_ref[tile] * jnp.dot(carry_ref[...], state, preferred_element_type=F32)
            gated = mixed * silu_ref[tile]
            gated_ref[tile] = gated
            square = square + gated * gated
        return square

    square = finish(core, jnp.zeros((TOK, 128), F32))
    remote(other_ref, state_ref.at[theirs_half], ex_send.at[2], ex_recv.at[2], {"ctx": partner}).wait_recv()
    square = finish(1 - core, square)
    norm = lax.rsqrt(jnp.sum(square, axis=1, keepdims=True) * (1.0 / COLS) + 1e-05)
    for t in range(TILES):
        sl = slice(128 * t, 128 * t + 128)
        mamba_ref[:, sl] = (gated_ref[t] * norm * gain_ref[:, sl]).astype(BF16)

    ex_state.wait_send()
    ex_thr.wait_send()
    ex_back.wait_send()

    def sent(k, _):
        s1(peer(k), z).wait_send()
        t1(peer(k), z).wait_send()
        s2(peer(k), z).wait_send()
        return 0

    lax.fori_loop(0, CHIPS - 1, sent, 0)

    @pl.when(z + HOP < CHIPS)
    def _():
        leap(0).wait_send()
        leap(1).wait_send()

    @pl.when(z + NEAR < CHIPS - 1)
    def _():
        round_back(0).wait_send()
        round_back(1).wait_send()

    def relayed(d, _):
        @pl.when(z >= d)
        def _():
            @pl.when((d < NEAR) & (d != HOP - 1) & (z < CHIPS - 1))
            def _():
                forward(d, 0).wait_send()
                forward(d, 1).wait_send()

            @pl.when(d > NEAR + 1)
            def _():
                backward(d, 0).wait_send()
                backward(d, 1).wait_send()

            pair(d).wait_send()

        return 0

    lax.fori_loop(0, FAR + 1, relayed, 0)


def per_device(
    mamba_input,
    mamba_gate,
    state_write,
    state_read,
    step_size,
    decay_rate,
    skip_scale,
    norm_gain,
    query_rows,
    key_rows,
    value_rows,
    doc_offsets,
):
    vmem, hbm = pl.BlockSpec(memory_space=pltpu.VMEM), pl.BlockSpec(memory_space=pl.ANY)
    dma = pltpu.SemaphoreType.DMA
    heads = query_rows.shape[1] // HD
    return pl.pallas_call(
        kernel,
        out_shape=(
            pltpu.VMEM(mamba_input.shape, BF16),
            pltpu.VMEM(query_rows.shape, BF16),
        ),
        in_specs=[pl.BlockSpec(memory_space=pltpu.SMEM)] + [vmem] * 4 + [hbm] * 7,
        out_specs=(vmem, vmem),
        scratch_shapes=[
            pltpu.VMEM((TOK, COLS), BF16),
            pltpu.VMEM((TOK, COLS), BF16),
            pltpu.VMEM((TOK, 128), BF16),
            pltpu.VMEM((TOK, 128), BF16),
            pltpu.VMEM((TOK, heads * HD), BF16),
            pltpu.VMEM((FAR + 1, 2, 2, TOK, HD), BF16),
            pltpu.VMEM((TOK, COLS), BF16),
            pltpu.VMEM((TOK, 128), BF16),
            pltpu.VMEM((TILES, TOK, 128), F32),
            pltpu.VMEM((TILES, TOK, 128), F32),
            pltpu.VMEM((TILES, TOK, 128), F32),
            pltpu.VMEM((32, 32, 128), F32),
            pltpu.VMEM((32, 32, 128), BF16),
            pltpu.VMEM((16, 32, 128), BF16),
            pltpu.VMEM((TILES, 1, 128), F32),
            pltpu.VMEM((TILES, 1, 128), F32),
            pltpu.VMEM((CHIPS, 32, 128), BF16),
            pltpu.VMEM((CHIPS, 1, 128), F32),
            pltpu.VMEM((CHIPS, 32, 128), BF16),
            pltpu.VMEM((CHIPS, 1, 128), F32),
            pltpu.VMEM((CHIPS, 32, 128), BF16),
            pltpu.VMEM((CHIPS, 32, 128), BF16),
            pltpu.VMEM((32, 32, 128), BF16),
            pltpu.VMEM((16, 32, 128), BF16),
            pltpu.VMEM((TOK, 128), jnp.int32),
            pltpu.VMEM((TOK, 128), jnp.int32),
            pltpu.VMEM((heads, TOK, 128), F32),
            pltpu.VMEM((heads, TOK, 256), F32),
            pltpu.VMEM((TILES, TOK, 128), F32),
            dma((7,)),
            dma((FAR + 1, 2)),
            dma((FAR + 1,)),
            dma((FAR + 3, 2)),
            dma((FAR + 1,)),
            dma((3,)),
            dma((3,)),
            dma((CHIPS,)),
            dma((CHIPS,)),
            dma((CHIPS,)),
            dma((CHIPS,)),
            dma((CHIPS,)),
            dma((CHIPS,)),
        ],
        compiler_params=pltpu.CompilerParams(collective_id=0, has_side_effects=True),
    )(
        doc_offsets,
        step_size.T,
        decay_rate.reshape(1, -1),
        skip_scale.reshape(1, -1),
        norm_gain.reshape(1, -1),
        mamba_input,
        mamba_gate,
        state_write,
        state_read,
        query_rows,
        key_rows,
        value_rows,
    )


def solution(mesh):
    rows, cols = P(("dp", "ctx"), "tensor"), P("tensor")
    return jax.shard_map(
        per_device,
        mesh=mesh,
        in_specs=(rows,) * 5 + (cols,) * 3 + (rows,) * 3 + (P("dp"),),
        out_specs=(rows, rows),
        check_vma=False,
    )
```

```python
import functools
import math

import jax
import jax.numpy as jnp
from jax import lax
from jax.experimental import pallas as pl
from jax.experimental.pallas import tpu as pltpu
from jax.sharding import PartitionSpec as P

MESH = pl.DeviceIdType.MESH
HIGHEST = lax.Precision.HIGHEST
F32, BF16 = jnp.float32, jnp.bfloat16

MP = 64
HD = 128
TOK = 128
CHIPS = 16
HEADS = 16
COLS = HEADS * MP
TILES = COLS // 128
HOP = 5
NEAR = 8
FAR = 12
STEPS = max(HOP - 1, NEAR - HOP + 1, FAR - NEAR) + 1
NEG = -1e30
SCALE = math.log2(math.e) / math.sqrt(HD)


def nt_dot(a, b):
    return lax.dot_general(a, b, (((1,), (1,)), ((), ())), preferred_element_type=F32)


def tn_dot(a, b):
    return lax.dot_general(a, b, (((0,), (0,)), ((), ())), preferred_element_type=F32)


def spread(table, tile):
    rows = table.shape[0]
    lane = lax.broadcasted_iota(jnp.int32, (rows, 128), 1)
    return jnp.where(lane < MP, table[:, 2 * tile : 2 * tile + 1], table[:, 2 * tile + 1 : 2 * tile + 2])


def kernel(
    offs_ref,
    step_ref,
    rate_ref,
    skip_ref,
    gain_ref,
    x_hbm,
    gate_hbm,
    write_hbm,
    read_hbm,
    q_hbm,
    k_hbm,
    v_hbm,
    mamba_ref,
    attn_ref,
    x_ref,
    gate_ref,
    b_ref,
    c_ref,
    q_ref,
    kv_ref,
    u_ref,
    carry_ref,
    er_ref,
    base_ref,
    silu_ref,
    own_ref,
    own_send,
    part_ref,
    thr_own,
    thr_part,
    comb_ref,
    comb_thr,
    in1_ref,
    thr1_ref,
    pre_ref,
    in2_ref,
    state_ref,
    other_ref,
    start_ref,
    qpos_ref,
    top_ref,
    acc_ref,
    gated_ref,
    load_sem,
    near_recv,
    pair_recv,
    near_send,
    pair_send,
    ex_send,
    ex_recv,
    s1_send,
    s1_recv,
    t1_send,
    t1_recv,
    s2_send,
    s2_recv,
):
    me = lax.axis_index("ctx")
    z, core = lax.div(me, 2), lax.rem(me, 2)
    partner = me + 1 - 2 * core
    anchor = me * TOK

    def chip(index):
        return {"ctx": 2 * index + core}

    def remote(src, dst, send, recv, device):
        return pltpu.make_async_remote_copy(
            src_ref=src, dst_ref=dst, send_sem=send, recv_sem=recv, device_id=device, device_id_type=MESH
        )

    def peer(k):
        turn = lax.div(k + 1, 2)
        away = CHIPS // 2 + jnp.where(lax.rem(k, 2) == 1, turn, -turn)
        return lax.rem(z + away, CHIPS)

    barrier = pltpu.get_barrier_semaphore()

    def greet(k, _):
        pl.semaphore_signal(barrier, inc=1, device_id=chip(peer(k)), device_id_type=MESH)
        return 0

    lax.fori_loop(0, CHIPS - 1, greet, 0)
    pl.semaphore_signal(barrier, inc=1, device_id={"ctx": partner}, device_id_type=MESH)

    loads = [
        pltpu.make_async_copy(src, dst, load_sem.at[n])
        for n, (src, dst) in enumerate(
            (
                (write_hbm, b_ref),
                (x_hbm, x_ref),
                (k_hbm, kv_ref.at[0, core, 0]),
                (v_hbm, kv_ref.at[0, core, 1]),
                (read_hbm, c_ref),
                (q_hbm, q_ref),
                (gate_hbm, gate_ref),
            )
        )
    ]
    for load in loads:
        load.start()

    row = lax.broadcasted_iota(jnp.int32, (TOK, 128), 0)
    col = lax.broadcasted_iota(jnp.int32, (TOK, 128), 1)
    pos = anchor + row
    start = jnp.zeros((TOK, 128), jnp.int32)
    final = jnp.zeros((8, 128), jnp.int32)
    for d in range(1, 32):
        off = offs_ref[d]
        start = jnp.where(pos >= off, off, start)
        final = jnp.where(anchor + TOK - 1 + jnp.zeros((8, 128), jnp.int32) >= off, off, final)
    final = final[0:1]
    start_ref[...] = start
    qpos_ref[...] = pos

    sums = jnp.concatenate([(col <= row).astype(F32), (col == row).astype(F32)], axis=0)
    sums = lax.dot_general(
        sums, step_ref[...], (((1,), (1,)), ((), ())), precision=HIGHEST, preferred_element_type=F32
    )
    running = -rate_ref[...] * sums[0:TOK]
    grow = jnp.exp(-running) * sums[TOK : 2 * TOK]
    er = jnp.exp(running)
    last = jnp.exp(running[TOK - 1 : TOK])

    for load in loads[:2]:
        load.wait()
    held = jnp.where(pos >= final, b_ref[...].astype(F32), 0.0)
    held_t = held.T.astype(BF16)
    for t in range(TILES):
        sl = slice(128 * t, 128 * t + 128)
        u = (x_ref[:, sl].astype(F32) * spread(grow, t)).astype(BF16)
        u_ref[:, sl] = u
        decay = spread(last, t)
        tile = jnp.dot(held_t, u, preferred_element_type=F32) * decay
        own_ref[4 * t : 4 * t + 4] = tile.reshape(4, 32, 128)
        own_send[4 * t : 4 * t + 4] = tile.astype(BF16).reshape(4, 32, 128)
        thr_own[t] = jnp.where(final < anchor, decay, 0.0)

    for load in loads[2:4]:
        load.wait()
    pl.semaphore_wait(barrier, CHIPS)

    def hop(d, e, part, sem, device):
        return remote(
            kv_ref.at[d, core, part], kv_ref.at[e, core, part], near_send.at[sem, part], near_recv.at[e, part], device
        )

    def forward(d, part):
        return hop(d, d + 1, part, d, chip(z + 1))

    def backward(d, part):
        return hop(d, d - 1, part, d, chip(z - 1))

    def leap(part):
        return hop(0, HOP, part, FAR + 1, chip(z + HOP))

    def round_back(part):
        target = jnp.minimum(z + FAR, CHIPS - 1)
        return hop(0, target - z, part, FAR + 2, chip(target))

    def pair(d):
        return remote(kv_ref.at[d, core], kv_ref.at[d, core], pair_send.at[d], pair_recv.at[d], {"ctx": partner})

    @pl.when(z < CHIPS - 1)
    def _():
        forward(0, 0).start()
        forward(0, 1).start()

    pair(0).start()

    ex_state = remote(
        own_send.at[pl.ds(16 * (1 - core), 16)], part_ref, ex_send.at[0], ex_recv.at[0], {"ctx": partner}
    )
    ex_thr = remote(thr_own, thr_part, ex_send.at[1], ex_recv.at[1], {"ctx": partner})
    ex_state.start()
    ex_thr.start()
    ex_thr.wait_recv()
    ex_state.wait_recv()
    is_first = core == 0
    for t in range(4):
        own = own_ref[pl.ds(16 * core + 4 * t, 4)]
        part = part_ref[4 * t : 4 * t + 4].astype(F32)
        mine, theirs = thr_own[4 * core + t], thr_part[4 * core + t]
        early, late = jnp.where(is_first, own, part), jnp.where(is_first, part, own)
        comb = jnp.where(is_first, theirs, mine)[None] * early + late
        comb_ref[4 * t : 4 * t + 4] = comb.astype(BF16)
        comb_thr[4 * t : 4 * t + 4] = jnp.broadcast_to((mine * theirs)[None], (4, 1, 128))

    def s1(target, source):
        return remote(comb_ref.at[target], in1_ref.at[source], s1_send.at[target], s1_recv.at[source], chip(target))

    def t1(target, source):
        return remote(comb_thr.at[target], thr1_ref.at[source], t1_send.at[target], t1_recv.at[source], chip(target))

    def s2(target, source):
        return remote(pre_ref.at[target], in2_ref.at[source], s2_send.at[target], s2_recv.at[source], chip(target))

    def send1(k, _):
        s1(peer(k), z).start()
        t1(peer(k), z).start()
        return 0

    lax.fori_loop(0, CHIPS - 1, send1, 0)

    @pl.when(z + NEAR < CHIPS - 1)
    def _():
        round_back(0).start()
        round_back(1).start()

    @pl.when(z + HOP < CHIPS)
    def _():
        leap(0).start()
        leap(1).start()

    in1_ref[z] = comb_ref[z]
    thr1_ref[z] = comb_thr[z]

    for load in loads[4:]:
        load.wait()
    top_ref[...] = jnp.full(top_ref.shape, NEG, F32)
    acc_ref[...] = jnp.zeros(acc_ref.shape, F32)
    heads = q_ref.shape[1] // HD

    def attend(d, causal):
        keys = jnp.concatenate([kv_ref[d, 0, 0], kv_ref[d, 1, 0]], axis=0)
        values = jnp.concatenate([kv_ref[d, 0, 1], kv_ref[d, 1, 1]], axis=0)
        values = jnp.concatenate([values, jnp.ones((2 * TOK, 128), BF16)], axis=1)
        lane = (z - d) * (2 * TOK) + lax.broadcasted_iota(jnp.int32, (TOK, 2 * TOK), 1)
        begin = start_ref[...]
        seen = lane >= jnp.concatenate([begin, begin], axis=1)
        if causal:
            here = qpos_ref[...]
            seen = seen & (lane <= jnp.concatenate([here, here], axis=1))
        for h in range(heads):
            scores = nt_dot(q_ref[:, h * HD : (h + 1) * HD], keys) * SCALE
            scores = jnp.where(seen, scores, NEG)
            before = top_ref[h]
            top = jnp.maximum(before, jnp.max(scores, axis=1, keepdims=True))
            top_ref[h] = top
            fade = jnp.exp2(before - top)
            weights = jnp.exp2(scores - jnp.concatenate([top, top], axis=1)).astype(BF16)
            update = jnp.dot(weights, values, preferred_element_type=F32)
            acc_ref[h] = acc_ref[h] * jnp.concatenate([fade, fade], axis=1) + update

    pair(0).wait_recv()
    attend(0, True)

    inner = jnp.where((col <= row) & (anchor + col >= start), nt_dot(c_ref[...], b_ref[...]), 0.0).astype(BF16)
    carry_ref[...] = jnp.where(start < anchor, c_ref[...].astype(F32), 0.0).astype(BF16)
    skip = skip_ref[...]
    for t in range(TILES):
        sl = slice(128 * t, 128 * t + 128)
        decay = spread(er, t)
        er_ref[t] = decay
        base_ref[t] = jnp.dot(inner, u_ref[:, sl], preferred_element_type=F32) * decay + spread(skip, t) * x_ref[
            :, sl
        ].astype(F32)
        gate = gate_ref[:, sl].astype(F32)
        silu_ref[t] = gate / (1.0 + jnp.exp(-gate))

    def scan():
        def arrive(k, _):
            s1(z, peer(k)).wait_recv()
            t1(z, peer(k)).wait_recv()
            return 0

        lax.fori_loop(0, CHIPS - 1, arrive, 0)
        prefix = jnp.zeros((32, 128), F32)
        for j in range(CHIPS):
            pre_ref[j] = prefix.astype(BF16)
            prefix = thr1_ref[j] * prefix + in1_ref[j].astype(F32)

        def send2(k, _):
            s2(peer(k), z).start()
            return 0

        lax.fori_loop(0, CHIPS - 1, send2, 0)
        in2_ref[z] = pre_ref[z]

    def block(d):
        pair(d).wait_recv()
        attend(d, False)

    def near_arrive(d):
        @pl.when(z >= d)
        def _():
            for part in range(2):
                hop(d, d, part, d, chip(z - d)).wait_recv()

                @pl.when((d < NEAR) & (d != HOP - 1) & (z < CHIPS - 1))
                def _(part=part):
                    forward(d, part).start()

                @pl.when(d > NEAR + 1)
                def _(part=part):
                    backward(d, part).start()

            pair(d).start()

    def step(n, _):
        @pl.when(n < HOP)
        def _():
            near_arrive(n)

        @pl.when(n == 1)
        def _():
            scan()

        @pl.when(n + HOP - 1 <= NEAR)
        def _():
            near_arrive(n + HOP - 1)

        @pl.when(FAR + 1 - n > NEAR)
        def _():
            near_arrive(FAR + 1 - n)

        def late(i, _):
            e = jnp.where(i == 0, n - 1, jnp.where(i == 1, n + HOP - 2, FAR + 2 - n))
            inside = jnp.where(i == 0, e < HOP, jnp.where(i == 1, e <= NEAR, e > NEAR))

            @pl.when(inside & (z >= e))
            def _():
                block(e)

            return 0

        @pl.when(n > 1)
        def _():
            lax.fori_loop(0, 3, late, 0)

        return 0

    lax.fori_loop(1, STEPS + 1, step, 0)

    def arrive2(k, _):
        s2(z, peer(k)).wait_recv()
        return 0

    lax.fori_loop(0, CHIPS - 1, arrive2, 0)
    for t in range(4):
        own = own_ref[pl.ds(16 * core + 4 * t, 4)]
        part = part_ref[4 * t : 4 * t + 4].astype(F32)
        mine, theirs = thr_own[4 * core + t], thr_part[4 * core + t]
        chip_in = in2_ref[4 * t : 4 * t + 4].astype(F32)
        second = jnp.where(is_first, mine, theirs)[None] * chip_in + jnp.where(is_first, own, part)
        state_ref[pl.ds(16 * core + 4 * t, 4)] = jnp.where(is_first, chip_in, second).astype(BF16)
        other_ref[4 * t : 4 * t + 4] = jnp.where(is_first, second, chip_in).astype(BF16)
    half = pl.ds(16 * core, 16)
    theirs_half = pl.ds(16 * (1 - core), 16)
    ex_back = remote(other_ref, state_ref.at[half], ex_send.at[2], ex_recv.at[2], {"ctx": partner})
    ex_back.start()
    for h in range(heads):
        attn_ref[:, h * HD : (h + 1) * HD] = (acc_ref[h, :, 0:HD] / acc_ref[h, :, HD : 2 * HD]).astype(BF16)

    def finish(side, square):
        for t in range(4):
            tile = 4 * side + t
            state = state_ref[pl.ds(4 * tile, 4)].reshape(128, 128)
            mixed = base_ref[tile] + er_ref[tile] * jnp.dot(carry_ref[...], state, preferred_element_type=F32)
            gated = mixed * silu_ref[tile]
            gated_ref[tile] = gated
            square = square + gated * gated
        return square

    square = finish(core, jnp.zeros((TOK, 128), F32))
    remote(other_ref, state_ref.at[theirs_half], ex_send.at[2], ex_recv.at[2], {"ctx": partner}).wait_recv()
    square = finish(1 - core, square)
    norm = lax.rsqrt(jnp.sum(square, axis=1, keepdims=True) * (1.0 / COLS) + 1e-05)
    for t in range(TILES):
        sl = slice(128 * t, 128 * t + 128)
        mamba_ref[:, sl] = (gated_ref[t] * norm * gain_ref[:, sl]).astype(BF16)

    ex_state.wait_send()
    ex_thr.wait_send()
    ex_back.wait_send()

    def sent(k, _):
        s1(peer(k), z).wait_send()
        t1(peer(k), z).wait_send()
        s2(peer(k), z).wait_send()
        return 0

    lax.fori_loop(0, CHIPS - 1, sent, 0)

    @pl.when(z + HOP < CHIPS)
    def _():
        leap(0).wait_send()
        leap(1).wait_send()

    @pl.when(z + NEAR < CHIPS - 1)
    def _():
        round_back(0).wait_send()
        round_back(1).wait_send()

    def relayed(d, _):
        @pl.when(z >= d)
        def _():
            @pl.when((d < NEAR) & (d != HOP - 1) & (z < CHIPS - 1))
            def _():
                forward(d, 0).wait_send()
                forward(d, 1).wait_send()

            @pl.when(d > NEAR + 1)
            def _():
                backward(d, 0).wait_send()
                backward(d, 1).wait_send()

            pair(d).wait_send()

        return 0

    lax.fori_loop(0, FAR + 1, relayed, 0)


def per_device(
    mamba_input,
    mamba_gate,
    state_write,
    state_read,
    step_size,
    decay_rate,
    skip_scale,
    norm_gain,
    query_rows,
    key_rows,
    value_rows,
    doc_offsets,
):
    vmem, hbm = pl.BlockSpec(memory_space=pltpu.VMEM), pl.BlockSpec(memory_space=pl.ANY)
    dma = pltpu.SemaphoreType.DMA
    heads = query_rows.shape[1] // HD
    return pl.pallas_call(
        kernel,
        out_shape=(
            pltpu.VMEM(mamba_input.shape, BF16),
            pltpu.VMEM(query_rows.shape, BF16),
        ),
        in_specs=[pl.BlockSpec(memory_space=pltpu.SMEM)] + [vmem] * 4 + [hbm] * 7,
        out_specs=(vmem, vmem),
        scratch_shapes=[
            pltpu.VMEM((TOK, COLS), BF16),
            pltpu.VMEM((TOK, COLS), BF16),
            pltpu.VMEM((TOK, 128), BF16),
            pltpu.VMEM((TOK, 128), BF16),
            pltpu.VMEM((TOK, heads * HD), BF16),
            pltpu.VMEM((FAR + 1, 2, 2, TOK, HD), BF16),
            pltpu.VMEM((TOK, COLS), BF16),
            pltpu.VMEM((TOK, 128), BF16),
            pltpu.VMEM((TILES, TOK, 128), F32),
            pltpu.VMEM((TILES, TOK, 128), F32),
            pltpu.VMEM((TILES, TOK, 128), F32),
            pltpu.VMEM((32, 32, 128), F32),
            pltpu.VMEM((32, 32, 128), BF16),
            pltpu.VMEM((16, 32, 128), BF16),
            pltpu.VMEM((TILES, 1, 128), F32),
            pltpu.VMEM((TILES, 1, 128), F32),
            pltpu.VMEM((CHIPS, 32, 128), BF16),
            pltpu.VMEM((CHIPS, 1, 128), F32),
            pltpu.VMEM((CHIPS, 32, 128), BF16),
            pltpu.VMEM((CHIPS, 1, 128), F32),
            pltpu.VMEM((CHIPS, 32, 128), BF16),
            pltpu.VMEM((CHIPS, 32, 128), BF16),
            pltpu.VMEM((32, 32, 128), BF16),
            pltpu.VMEM((16, 32, 128), BF16),
            pltpu.VMEM((TOK, 128), jnp.int32),
            pltpu.VMEM((TOK, 128), jnp.int32),
            pltpu.VMEM((heads, TOK, 128), F32),
            pltpu.VMEM((heads, TOK, 256), F32),
            pltpu.VMEM((TILES, TOK, 128), F32),
            dma((7,)),
            dma((FAR + 1, 2)),
            dma((FAR + 1,)),
            dma((FAR + 3, 2)),
            dma((FAR + 1,)),
            dma((3,)),
            dma((3,)),
            dma((CHIPS,)),
            dma((CHIPS,)),
            dma((CHIPS,)),
            dma((CHIPS,)),
            dma((CHIPS,)),
            dma((CHIPS,)),
        ],
        compiler_params=pltpu.CompilerParams(collective_id=0, has_side_effects=True),
    )(
        doc_offsets,
        step_size.T,
        decay_rate.reshape(1, -1),
        skip_scale.reshape(1, -1),
        norm_gain.reshape(1, -1),
        mamba_input,
        mamba_gate,
        state_write,
        state_read,
        query_rows,
        key_rows,
        value_rows,
    )


def solution(mesh):
    rows, cols = P(("dp", "ctx"), "tensor"), P("tensor")
    return jax.shard_map(
        per_device,
        mesh=mesh,
        in_specs=(rows,) * 5 + (cols,) * 3 + (rows,) * 3 + (P("dp"),),
        out_specs=(rows, rows),
        check_vma=False,
    )
```
